32 devices in a mesh: tx: 2 (over core), ty: 16 (over z, y, x).
Axes of the slice: x: 2, y: 2, z: 4, core: 2. Of those that a mesh axis runs over, the one named last changes fastest.
Arguments:
- handoff: int32 [2, 16, 48, 1], P('tx', 'ty'), may hold values from 0 to 8, as said below
- cells: int32 [2, 16, 48, 128], P('tx', 'ty'), may hold values from 0 to 32767
- offsets: int32 [2, 16, 48, 3, 128], P('tx', 'ty'), may hold values from 0 to 15
- drag: float32 [2, 16, 48, 3, 128], P('tx', 'ty'), may hold values from -6 to 6
- bubble_velocity: float32 [2, 16, 48, 3, 128], P('tx', 'ty'), may hold values from -6 to 6
- gas: float32 [3, 32, 256, 128], P(None, 'tx', 'ty'), may hold values from -6 to 6
Outputs:
- gas_new: float32 [3, 32, 256, 128], P(None, 'tx', 'ty')
- slip: float32 [2, 16, 64, 3, 128], P('tx', 'ty')
The draws below stay inside these ranges and needn't reach their ends.
Inputs may be any that keep to these rules, and one draw needn't show every extreme that they name: `handoff`: of one tile's 48 blocks at most 2 carry the same code other than 4, and in every draw some tile has exactly 2 blocks with one such code. How many blocks keep code 4 varies from tile to tile. `cells`: linear index ix * 16 * 128 + iy * 128 + iz of the bubble's cell within the tile that holds its block after the handoff. `offsets`: position of the bubble inside its cell along each dimension, in sixteenths.
All inputs are finite; a program needn't handle non-finite values.
Results may differ from the reference program's by a relative error of at most 0.0003.
Values sent between devices are 32-bit elements; how exact they have to be, the bound alone decides.
No kernel may reach another device: no remote copies, remote signals or barrier semaphores. Data moves between devices by JAX's collectives and lax.ppermute only.
A program may use at most 64 MiB of HBM per device.

```python
import jax
import jax.numpy as jnp

CX = 16
CY = 16
NZ = 128
SLOTS = 48
BUB = 128
SWEEPS = 4
CAP = 2
TILES_X = 2
TILES_Y = 16
NX = 32
NY = 256


def draw_handoff(key, part):
    base = jax.random.fold_in(key, 7301)
    key_leave, key_code, key_forced, key_rate = jax.random.split(base, 4)
    shape = (TILES_X, TILES_Y, SLOTS)
    rate = jax.random.randint(key_rate, (TILES_X, TILES_Y, 1), 1, 9)
    leaving = jax.random.randint(key_leave, shape, 0, 20) < rate
    raw = jax.random.randint(key_code, shape, 0, 8)
    codes = raw + (raw >= 4).astype(jnp.int32)
    codes = jnp.where(leaving, codes, 4)
    forced_raw = jax.random.randint(key_forced, (), 0, 8)
    forced = forced_raw + (forced_raw >= 4).astype(jnp.int32)
    tile_x = jnp.arange(TILES_X, dtype=jnp.int32)[:, None, None]
    tile_y = jnp.arange(TILES_Y, dtype=jnp.int32)[None, :, None]
    slot_id = jnp.arange(SLOTS, dtype=jnp.int32)[None, None, :]
    pinned = (tile_x == 0) & (tile_y == 0) & (slot_id < CAP)
    codes = jnp.where(pinned, forced, codes)
    matches = (codes[..., None] == jnp.arange(9, dtype=jnp.int32)).astype(jnp.int32)
    rank_in = jnp.sum((jnp.cumsum(matches, axis=2) - 1) * matches, axis=3)
    codes = jnp.where((codes != 4) & (rank_in >= CAP), 4, codes)
    return codes.astype(jnp.int32)[..., None]


def place_ends(drawn, own_key, least, high):
    index_at = [jax.random.randint(jax.random.fold_in(own_key, axis), (), 0, length) for axis, length in enumerate(drawn.shape)]
    widest = drawn.shape.index(max(drawn.shape))
    beside = index_at[:widest] + [(index_at[widest] + 1) % drawn.shape[widest]] + index_at[widest + 1:]
    return drawn.at[tuple(index_at)].set(least).at[tuple(beside)].set(high)


def block_levels(rng, shape, cuts, least, top_value):
    level = 1.0
    for axis_at, blocks in cuts:
        steps = jax.random.uniform(jax.random.fold_in(jax.random.fold_in(rng, 6), axis_at), (blocks,), jnp.float32, least / len(cuts), top_value / len(cuts))
        level = level * jnp.repeat(jnp.exp(steps), shape[axis_at] // blocks).reshape((-1,) + (1,) * (len(shape) - 1 - axis_at))
    return level


def noise(own_key, dims, spread, most, pieces=(), held_as=jnp.bfloat16):
    result = spread * jax.random.normal(own_key, dims, jnp.float32)
    if pieces:
        result = result * block_levels(own_key, dims, pieces, -0.22, 0.18)
    return jnp.clip(result, -most, most).astype(held_as)


def setup_inputs(seed: int = 0) -> dict:
    seeds = jax.random.split(jax.random.key(seed), 7)
    handoff = draw_handoff(jax.random.fold_in(seeds[6], 71), 0)
    cells = place_ends(jax.random.randint(seeds[1], (TILES_X, TILES_Y, SLOTS, BUB), 0, CX * CY * NZ), jax.random.fold_in(seeds[1], 1), 0, (CX * CY * NZ) - 1).astype(jnp.int32)
    offsets = place_ends(jax.random.randint(seeds[2], (TILES_X, TILES_Y, SLOTS, 3, BUB), 0, 16), jax.random.fold_in(seeds[2], 1), 0, 15).astype(jnp.int32)
    drag = noise(seeds[3], (TILES_X, TILES_Y, SLOTS, 3, BUB), 1.0, 6.0, ((0, 2), (1, 16)), jnp.float32)
    bubble_velocity = noise(seeds[4], (TILES_X, TILES_Y, SLOTS, 3, BUB), 1.0, 6.0, ((0, 2), (1, 16)), jnp.float32)
    gas = noise(seeds[5], (3, NX, NY, NZ), 1.0, 6.0, ((1, 2), (2, 16)), jnp.float32)
    return {"handoff": handoff, "cells": cells, "offsets": offsets, "drag": drag, "bubble_velocity": bubble_velocity, "gas": gas}


DIFFUSE = 1.0
STEP_SIZE = 2.0


def tsc_weights(sixteenths):
    fraction = (sixteenths.astype(jnp.float32) + 0.5) / 16.0 - 0.5
    return (0.5 * (0.5 - fraction) ** 2, 0.75 - fraction * fraction, 0.5 * (0.5 + fraction) ** 2)


def reference(handoff, cells, offsets, drag, bubble_velocity, gas):
    tiles_x, tiles_y, slot_count = handoff.shape[0], handoff.shape[1], handoff.shape[2]
    per_block = cells.shape[3]
    cells_x, cells_y, column_depth = gas.shape[1], gas.shape[2], gas.shape[3]
    width_x = cells_x // tiles_x
    width_y = cells_y // tiles_y
    dest_codes = handoff[:, :, :, 0]
    matches = (dest_codes[..., None] == jnp.arange(9, dtype=jnp.int32)).astype(jnp.int32)
    rank_in = jnp.sum((jnp.cumsum(matches, axis=2).astype(jnp.int32) - 1) * matches, axis=3).astype(jnp.int32)
    rank_in = jnp.where(dest_codes == 4, CAP, rank_in).astype(jnp.int32)
    tile_x = jnp.broadcast_to(jnp.arange(tiles_x, dtype=jnp.int32)[:, None, None], dest_codes.shape)
    tile_y = jnp.broadcast_to(jnp.arange(tiles_y, dtype=jnp.int32)[None, :, None], dest_codes.shape)
    payload = jnp.concatenate([drag, bubble_velocity], axis=3)
    integers = jnp.concatenate([cells[:, :, :, None, :], offsets], axis=3)
    out_float = jnp.zeros((tiles_x, tiles_y, 9, CAP, 6, per_block), jnp.float32)
    out_float = out_float.at[tile_x, tile_y, dest_codes, rank_in].set(payload, mode="drop")
    out_int = jnp.zeros((tiles_x, tiles_y, 9, CAP, 4, per_block), jnp.int32)
    out_int = out_int.at[tile_x, tile_y, dest_codes, rank_in].set(integers, mode="drop")
    out_live = jnp.zeros((tiles_x, tiles_y, 9, CAP), jnp.float32)
    out_live = out_live.at[tile_x, tile_y, dest_codes, rank_in].set(1.0, mode="drop")

    def arrive(outgoing):
        collected = []
        for source_group in range(9):
            if source_group == 4:
                continue
            step_x = source_group // 3 - 1
            step_y = source_group % 3 - 1
            collected.append(jnp.roll(outgoing[:, :, 8 - source_group], (-step_x, -step_y), axis=(0, 1)))
        stacked = jnp.stack(collected, axis=2)
        return stacked.reshape((tiles_x, tiles_y, 8 * CAP) + stacked.shape[4:])

    stay = (dest_codes == 4).astype(jnp.float32)
    received_f = jnp.concatenate([payload, arrive(out_float)], axis=2)
    received_i = jnp.concatenate([integers, arrive(out_int)], axis=2)
    occupied = jnp.concatenate([stay, arrive(out_live)], axis=2)
    cell_index = received_i[:, :, :, 0]
    base_x = (jnp.arange(tiles_x, dtype=jnp.int32) * width_x)[:, None, None, None]
    base_y = (jnp.arange(tiles_y, dtype=jnp.int32) * width_y)[None, :, None, None]
    global_x = base_x + cell_index // (width_y * column_depth)
    global_y = base_y + (cell_index // column_depth) % width_y
    global_z = cell_index % column_depth
    along = [tsc_weights(received_i[:, :, :, 1 + axis_id]) for axis_id in range(3)]
    live_flat = jnp.broadcast_to(occupied[..., None], cell_index.shape).reshape(-1)
    forces = jnp.moveaxis(received_f[:, :, :, 0:3], 3, 0).reshape(3, -1) * live_flat[None, :]
    total_cells = cells_x * cells_y * column_depth
    stencil = []
    for step_x in (-1, 0, 1):
        for step_y in (-1, 0, 1):
            for step_z in (-1, 0, 1):
                index = (((global_x + step_x) % cells_x) * cells_y + (global_y + step_y) % cells_y) * column_depth
                index = (index + (global_z + step_z) % column_depth).astype(jnp.int32).reshape(-1)
                weight = (along[0][step_x + 1] * along[1][step_y + 1] * along[2][step_z + 1]).reshape(-1)
                stencil.append((index, weight))
    deposited = jnp.zeros((3, total_cells), jnp.float32)
    for index, weight in stencil:
        deposited = deposited.at[:, index].add(forces * weight[None, :])
    source = deposited.reshape(3, cells_x, cells_y, column_depth)
    filtered = source
    for sweep in range(SWEEPS):
        beside_all = jnp.roll(filtered, 1, axis=1) + jnp.roll(filtered, -1, axis=1)
        beside_all = beside_all + jnp.roll(filtered, 1, axis=2) + jnp.roll(filtered, -1, axis=2)
        beside_all = beside_all + jnp.roll(filtered, 1, axis=3) + jnp.roll(filtered, -1, axis=3)
        filtered = (source + DIFFUSE * beside_all) / (1.0 + 6.0 * DIFFUSE)
    gas_new = gas + STEP_SIZE * filtered
    flat_gas = gas_new.reshape(3, -1)
    sampled = jnp.zeros((3, live_flat.shape[0]), jnp.float32)
    for index, weight in stencil:
        sampled = sampled + flat_gas[:, index] * weight[None, :]
    own_velocity = jnp.moveaxis(received_f[:, :, :, 3:6], 3, 0).reshape(3, -1)
    slip_flat = (sampled - own_velocity) * live_flat[None, :]
    slip = jnp.moveaxis(slip_flat.reshape((3,) + cell_index.shape), 0, 3)
    return gas_new, slip
```

```python
import functools

import jax
import jax.numpy as jnp
from jax import lax
from jax.experimental import pallas as pl
from jax.experimental.pallas import tpu as pltpu
from jax.sharding import PartitionSpec as P

SWEEPS = 4
CAP = 2
DIFFUSE = 1.0
STEP_SIZE = 2.0

REC = 16
STAY = 4
REACH = SWEEPS + 1
EDGE = REACH + 1
SUB = 8
VMEM = pl.BlockSpec(memory_space=pltpu.VMEM)
SMEM = pl.BlockSpec(memory_space=pltpu.SMEM)


def round_up(count, unit):
    return -(-count // unit) * unit


def call(body, outs, args, specs=None, scratch=(), aliases=None, cost=(0, 0), name=None):
    return pl.pallas_call(
        body,
        out_shape=[jax.ShapeDtypeStruct(shape, jnp.float32) for shape in outs],
        in_specs=specs or [VMEM] * len(args),
        out_specs=[VMEM] * len(outs),
        scratch_shapes=list(scratch),
        input_output_aliases=aliases or {},
        cost_estimate=pl.CostEstimate(flops=cost[0], bytes_accessed=cost[1], transcendentals=0),
        name=name,
    )(*args)


def split_by(value, size):
    if size & (size - 1) == 0:
        return value >> (size.bit_length() - 1), value & (size - 1)
    return value // size, value % size


class Tile:
    def __init__(self, wx, wy, nz):
        self.wx, self.wy, self.nz = wx, wy, nz
        self.ye = wy + 2
        self.hp = round_up(self.ye, SUB)
        self.main = self.ye * wx
        self.rows = self.main + 2 * self.hp
        self.yw = wy + 2 * REACH
        self.yp = round_up(self.yw, SUB)
        self.edge_main = EDGE * wx
        self.edge_rows = round_up(3 * (self.edge_main + 2 * EDGE), SUB)

    def decode(self, cell):
        cx, rest = split_by(cell, self.wy * self.nz)
        cy, cz = split_by(rest, self.nz)
        return cx, cy, cz

    def planar(self, cx, cy, weights):
        low, mid, high = weights
        lanes = cx.shape[1]
        ix = lax.broadcasted_iota(jnp.int32, (self.wx, lanes), 0)
        tx = jnp.where(ix == cx + 1, high[0:1], 0.0)
        tx = jnp.where(ix == cx, mid[0:1], tx)
        tx = jnp.where(ix == cx - 1, low[0:1], tx)
        iy = lax.broadcasted_iota(jnp.int32, (self.hp, lanes), 0)
        ty = jnp.where(iy == cy + 2, high[1:2], 0.0)
        ty = jnp.where(iy == cy + 1, mid[1:2], ty)
        ty = jnp.where(iy == cy, low[1:2], ty)
        beyond_low = jnp.where(cx == 0, low[0:1], 0.0)
        beyond_high = jnp.where(cx == self.wx - 1, high[0:1], 0.0)
        parts = [tx * ty[j : j + 1] for j in range(self.ye)]
        return parts + [ty * beyond_low, ty * beyond_high]

    def vertical(self, cz, weights):
        low, mid, high = weights
        iz = lax.broadcasted_iota(jnp.int32, (self.nz, cz.shape[1]), 0)
        below = jnp.where(cz == 0, self.nz - 1, cz - 1)
        above = jnp.where(cz == self.nz - 1, 0, cz + 1)
        tz = jnp.where(iz == above, high[2:3], 0.0)
        tz = jnp.where(iz == cz, mid[2:3], tz)
        return jnp.where(iz == below, low[2:3], tz)


def tsc_weights(sixteenths):
    fraction = (sixteenths + 0.5) * (1.0 / 16.0) - 0.5
    low = 0.5 - fraction
    high = 0.5 + fraction
    return 0.5 * low * low, 0.75 - fraction * fraction, 0.5 * high * high


def halves(value):
    top = value.astype(jnp.bfloat16)
    return top, (value - top.astype(jnp.float32)).astype(jnp.bfloat16)


def deposit_chunk(tile, blocks):
    left, right = [], []
    for cell, sixteenths, force in blocks:
        cx, cy, cz = tile.decode(cell)
        weights = tsc_weights(sixteenths)
        tops, lows = zip(*[halves(part) for part in tile.planar(cx, cy, weights)])
        left.append((jnp.concatenate(tops, axis=0), jnp.concatenate(lows, axis=0)))
        tz = tile.vertical(cz, weights)
        tops, lows = zip(*[halves(tz * force[k : k + 1]) for k in range(3)])
        right.append((jnp.concatenate(tops, axis=0), jnp.concatenate(lows, axis=0)))
    a_top, a_low = (jnp.concatenate(part, axis=1) for part in zip(*left))
    b_top, b_low = (jnp.concatenate(part, axis=1) for part in zip(*right))
    return lax.dot_general(
        jnp.concatenate([a_top, a_top, a_low], axis=1),
        jnp.concatenate([b_top, b_low, b_top], axis=1),
        (((1,), (1,)), ((), ())),
        preferred_element_type=jnp.float32,
    )


def ty_roles(axis, count):
    if count % 2:
        return True, False
    even = lax.axis_index(axis) % 2 == 0
    return even, even


def if_(cond, then, other):
    if isinstance(cond, bool):
        (then if cond else other)()
        return
    pl.when(cond)(then)
    pl.when(jnp.logical_not(cond))(other)


def pack_kernel(tile, slots, codes, cells, offsets, drag, velocity, gas, xsend, own, counts):
    xsend[:, : 3 * CAP] = jnp.zeros((2, 3 * CAP, REC, 128), jnp.float32)
    own[...] = jnp.zeros(own.shape, jnp.float32)
    for code in range(9):
        counts[code] = 0
    per = tile.wy // REC
    for k in range(3):
        for side, x in ((0, 0), (1, tile.wx - 1)):
            for part in range(per):
                start = (k * tile.wx + x) * tile.wy + part * REC
                xsend[side, 3 * CAP + k * per + part] = gas[start : start + REC]

    def visit(slot, carry):
        code = codes[slot]

        @pl.when(code != STAY)
        def _():
            rank = jnp.minimum(counts[code], CAP - 1)
            counts[code] = rank + 1

            def put(ref, side, place):
                ref[side, place, 0:3] = drag[slot]
                ref[side, place, 3:6] = velocity[slot]
                ref[side, place, 6:7] = cells[pl.ds(slot, 1)].astype(jnp.float32)
                ref[side, place, 7:10] = offsets[slot].astype(jnp.float32)
                ref[side, place, 10:11] = jnp.ones((1, 128), jnp.float32)

            step_x, step_y = code // 3, code % 3
            pl.when(step_x == 1)(lambda: put(own, step_y // 2, rank))
            pl.when(step_x != 1)(lambda: put(xsend, step_x // 2, step_y * CAP + rank))

        return carry

    lax.fori_loop(0, slots, visit, 0)


def join_kernel(tile, axis, count, xrecv, own, gas, send_a, send_b):
    a_high, _ = ty_roles(axis, count)
    per_x, per_y = tile.wx // REC, tile.wy // REC

    def fill(ref, high):
        step = 2 * CAP * int(high)
        y = tile.wy - 1 if high else 0
        for s in range(CAP):
            ref[s] = xrecv[1, step + s]
            ref[CAP + s] = own[int(high), s]
            ref[2 * CAP + s] = xrecv[0, step + s]
        for k in range(3):
            for part in range(per_x):
                start = (k * tile.wx + part * REC) * tile.wy + y
                ref[3 * CAP + k * per_x + part] = gas[pl.ds(start, REC, stride=tile.wy), :]
            place = 3 * CAP + k * per_y + y // REC
            corner = 3 * CAP + 3 * per_x
            ref[corner, 2 * k : 2 * k + 1] = xrecv[1, place, y % REC : y % REC + 1]
            ref[corner, 2 * k + 1 : 2 * k + 2] = xrecv[0, place, y % REC : y % REC + 1]

    def even():
        fill(send_a, True)
        fill(send_b, False)

    def odd():
        fill(send_a, False)
        fill(send_b, True)

    for ref in (send_a, send_b):
        ref[3 * CAP + 3 * per_x] = jnp.zeros((REC, 128), jnp.float32)
    if_(a_high, even, odd)


def own_kernel(tile, slots, codes, cells, offsets, drag, acc):
    acc[...] = jnp.zeros(acc.shape, jnp.float32)

    def step(pair, carry):
        blocks = []
        for i in range(2):
            slot = pair * 2 + i
            stays = (codes[slot] == STAY).astype(jnp.float32)
            blocks.append(
                (
                    cells[pl.ds(slot, 1)],
                    offsets[slot].astype(jnp.float32),
                    drag[slot] * stays,
                )
            )
        acc[...] += deposit_chunk(tile, blocks)
        return carry

    lax.fori_loop(0, slots // 2, step, 0)


ARRIVAL_LOW, ARRIVAL_HIGH = (0, 3, 5), (2, 4, 7)


def arrive_kernel(tile, axis, count, recv_a, recv_b, xrecv, acc_in, acc, arrivals, send_a, send_b):
    a_high, a_from_high = ty_roles(axis, count)
    for s in range(CAP):
        arrivals[1 * CAP + s] = xrecv[1, CAP + s]
        arrivals[6 * CAP + s] = xrecv[0, CAP + s]

    def place(ref, order):
        for i, j in enumerate(order):
            for s in range(CAP):
                arrivals[j * CAP + s] = ref[i * CAP + s]

    if_(
        a_from_high,
        lambda: (place(recv_a, ARRIVAL_HIGH), place(recv_b, ARRIVAL_LOW)) and None,
        lambda: (place(recv_a, ARRIVAL_LOW), place(recv_b, ARRIVAL_HIGH)) and None,
    )
    acc[...] = acc_in[...]

    def step(pair, carry):
        blocks = []
        for i in range(2):
            record = arrivals[pair * 2 + i]
            blocks.append(
                (
                    record[6:7].astype(jnp.int32),
                    record[7:10],
                    record[0:3] * record[10:11],
                )
            )
        acc[...] += deposit_chunk(tile, blocks)
        return carry

    lax.fori_loop(0, 8 * CAP // 2, step, 0)

    def edge(ref, high):
        first = tile.ye - EDGE if high else 0
        tail = 3 * tile.edge_main
        for k in range(3):
            lanes = slice(k * tile.nz, (k + 1) * tile.nz)
            ref[k * tile.edge_main : (k + 1) * tile.edge_main] = acc[
                first * tile.wx : (first + EDGE) * tile.wx, lanes
            ]
            for h in range(2):
                start = tile.main + h * tile.hp + first
                row = tail + (2 * k + h) * EDGE
                ref[row : row + EDGE] = acc[start : start + EDGE, lanes]

    def even():
        edge(send_a, True)
        edge(send_b, False)

    def odd():
        edge(send_a, False)
        edge(send_b, True)

    for ref in (send_a, send_b):
        last = tile.edge_rows - SUB
        ref[last:] = jnp.zeros((SUB, tile.nz), jnp.float32)
    if_(a_high, even, odd)


def widen_kernel(tile, axis, count, acc, recv_a, recv_b, mid, beyond, xsend):
    _, a_from_high = ty_roles(axis, count)
    own = slice(REACH - 1, REACH - 1 + tile.ye)
    for k in range(3):
        lanes = slice(k * tile.nz, (k + 1) * tile.nz)
        zero = jnp.zeros((REACH - 1, tile.wx, tile.nz), jnp.float32)
        mid[k, : REACH - 1] = zero
        mid[k, REACH - 1 + tile.ye :] = zero
        mid[k, own] = acc[: tile.main, lanes].reshape(tile.ye, tile.wx, tile.nz)
        for h in range(2):
            start = tile.main + h * tile.hp
            beyond[k, h] = jnp.zeros((tile.yp, tile.nz), jnp.float32)
            beyond[k, h, own] = acc[start : start + tile.ye, lanes]

    def add(ref, high):
        first = tile.yw - EDGE if high else 0
        tail = 3 * tile.edge_main
        for k in range(3):
            rows = ref[k * tile.edge_main : (k + 1) * tile.edge_main]
            mid[k, first : first + EDGE] += rows.reshape(EDGE, tile.wx, tile.nz)
            for h in range(2):
                row = tail + (2 * k + h) * EDGE
                beyond[k, h, first : first + EDGE] += ref[row : row + EDGE]

    if_(
        a_from_high,
        lambda: (add(recv_a, True), add(recv_b, False)) and None,
        lambda: (add(recv_a, False), add(recv_b, True)) and None,
    )
    tail = 3 * tile.yw
    for k in range(3):
        for side, first in ((0, 0), (1, tile.wx - SUB)):
            for y in range(tile.yw):
                xsend[side, k * tile.yw + y] = mid[k, y, first : first + SUB]
            for part in range(tile.yp // SUB):
                xsend[side, tail + k * (tile.yp // SUB) + part] = beyond[
                    k, side, part * SUB : (part + 1) * SUB
                ]


def finish_kernel(
    tile, axis, count, slots, codes, cells, offsets, velocity, gas, xgas, ygas_a, ygas_b,
    arrivals, mid, beyond, xrecv, gas_new, slip, src, ping, pong, field, stack,
):
    _, a_from_high = ty_roles(axis, count)
    wide = tile.wx + 2 * SUB
    tail = 3 * tile.yw
    parts = tile.yp // SUB
    for k in range(3):
        for y in range(tile.yw):
            place = tail + k * parts + y // SUB
            row = y % SUB
            src[k, y, 0:SUB] = xrecv[1, k * tile.yw + y]
            src[k, y, SUB : SUB + tile.wx] = mid[k, y]
            src[k, y, SUB + tile.wx :] = xrecv[0, k * tile.yw + y]
            src[k, y, SUB - 1 : SUB] += beyond[k, 0, y : y + 1]
            src[k, y, SUB + tile.wx : SUB + tile.wx + 1] += beyond[k, 1, y : y + 1]
            src[k, y, SUB : SUB + 1] += xrecv[1, place, row : row + 1]
            src[k, y, SUB + tile.wx - 1 : SUB + tile.wx] += xrecv[0, place, row : row + 1]

    def sweep(old, new, margin):
        def row(y, carry):
            for k in range(3):
                here = old[k, y]
                around = old[k, y - 1] + old[k, y + 1]
                around = around + pltpu.roll(here, 1, 0) + pltpu.roll(here, wide - 1, 0)
                around = around + pltpu.roll(here, 1, 1) + pltpu.roll(here, tile.nz - 1, 1)
                new[k, y] = (src[k, y] + DIFFUSE * around) * (1.0 / (1.0 + 6.0 * DIFFUSE))
            return carry

        lax.fori_loop(margin, tile.yw - margin, row, 0, unroll=2)

    buffers = [src, ping, pong, ping, pong]
    for index in range(SWEEPS):
        sweep(buffers[index], buffers[index + 1], index + 1)
    filtered = buffers[SWEEPS]

    per_x, per_y = tile.wx // REC, tile.wy // REC

    def take_edges(ref, high):
        y = tile.ye - 1 if high else 0
        for k in range(3):
            for part in range(per_x):
                row = y * tile.wx + part * REC
                stack[k, row : row + REC] = ref[3 * CAP + k * per_x + part]
            corner = 3 * CAP + 3 * per_x
            for h in range(2):
                row = tile.main + h * tile.hp + y
                stack[k, row : row + 1] = ref[corner, 2 * k + h : 2 * k + h + 1]

    for k in range(3):
        for h in range(2):
            start = tile.main + h * tile.hp
            stack[k, start : start + tile.hp] = jnp.zeros((tile.hp, tile.nz), jnp.float32)
            for part in range(per_y):
                row = start + 1 + part * REC
                stack[k, row : row + REC] = xgas[1 - h, 3 * CAP + k * per_y + part]
        for y in range(tile.wy):
            stack[k, (y + 1) * tile.wx : (y + 2) * tile.wx] = gas[
                pl.ds(k * tile.wx * tile.wy + y, tile.wx, stride=tile.wy), :
            ]
    if_(
        a_from_high,
        lambda: (take_edges(ygas_a, True), take_edges(ygas_b, False)) and None,
        lambda: (take_edges(ygas_a, False), take_edges(ygas_b, True)) and None,
    )
    depth = field.shape[1]
    for k in range(3):
        for y in range(tile.ye):
            rows = slice(y * tile.wx, (y + 1) * tile.wx)
            value = filtered[k, y + REACH - 1]
            updated = stack[k, rows] + STEP_SIZE * value[SUB : SUB + tile.wx]
            stack[k, rows] = updated
            if 1 <= y <= tile.wy:
                gas_new[pl.ds(k * tile.wx * tile.wy + y - 1, tile.wx, stride=tile.wy), :] = updated
            for h, x in ((0, SUB - 1), (1, SUB + tile.wx)):
                row = tile.main + h * tile.hp + y
                stack[k, row : row + 1] += STEP_SIZE * value[x : x + 1]
        whole = stack[k]
        top = whole.astype(jnp.bfloat16).astype(jnp.float32)
        pad = jnp.zeros((depth - 3 * tile.rows, tile.nz), jnp.float32)
        both = jnp.concatenate([top, top, whole - top, pad], axis=0)
        field[k * tile.nz : (k + 1) * tile.nz] = both.T.astype(jnp.bfloat16)

    def sample(blocks):
        tables, verticals = [], []
        for cell, sixteenths in blocks:
            cx, cy, cz = tile.decode(cell)
            weights = tsc_weights(sixteenths)
            tops, lows = zip(*[halves(part) for part in tile.planar(cx, cy, weights)])
            pad = jnp.zeros((depth - 3 * tile.rows, 128), jnp.bfloat16)
            tables.append(jnp.concatenate(tops + lows + tops + (pad,), axis=0))
            verticals.append(tile.vertical(cz, weights))
        column = jnp.dot(
            field[...], jnp.concatenate(tables, axis=1), preferred_element_type=jnp.float32
        )
        out = []
        for i, vertical in enumerate(verticals):
            part = column[:, i * 128 : (i + 1) * 128]
            sums = [
                jnp.sum(part[k * tile.nz : (k + 1) * tile.nz] * vertical, axis=0, keepdims=True)
                for k in range(3)
            ]
            out.append(jnp.concatenate(sums, axis=0))
        return out

    def own_step(pair, carry):
        first = pair * 2
        blocks = [(cells[pl.ds(first + i, 1)], offsets[first + i].astype(jnp.float32)) for i in range(2)]
        for i, value in enumerate(sample(blocks)):
            stays = (codes[first + i] == STAY).astype(jnp.float32)
            slip[first + i] = (value - velocity[first + i]) * stays
        return carry

    lax.fori_loop(0, slots // 2, own_step, 0)

    def arrival_step(pair, carry):
        first = pair * 2
        records = [arrivals[first + i] for i in range(2)]
        blocks = [(record[6:7].astype(jnp.int32), record[7:10]) for record in records]
        for i, value in enumerate(sample(blocks)):
            slip[slots + first + i] = (value - records[i][3:6]) * records[i][10:11]
        return carry

    lax.fori_loop(0, 8 * CAP // 2, arrival_step, 0)


def exchange_x(buffer, axis, count):
    forward = [(i, (i + 1) % count) for i in range(count)]
    backward = [(target, source) for source, target in forward]
    if count == 2:
        return lax.ppermute(buffer, axis, forward)
    return jnp.stack(
        [lax.ppermute(buffer[0], axis, backward), lax.ppermute(buffer[1], axis, forward)]
    )


def exchange_y(send_a, send_b, axis, count):
    if count % 2:
        perm_a = [(i, (i + 1) % count) for i in range(count)]
        perm_b = [(target, source) for source, target in perm_a]
    else:
        perm_a = [(i, i ^ 1) for i in range(count)]
        perm_b = [(i, (i + 1) % count if i % 2 else (i - 1) % count) for i in range(count)]
    return lax.ppermute(send_a, axis, perm_a), lax.ppermute(send_b, axis, perm_b)


def on_device(count_x, count_y, handoff, cells, offsets, drag, bubble_velocity, gas):
    tile = Tile(gas.shape[1], gas.shape[2], gas.shape[3])
    slots, lanes = cells.shape[2], cells.shape[3]
    codes = handoff.reshape(slots)
    cells = cells.reshape(slots, lanes)
    offsets = offsets.reshape(slots, 3, lanes)
    drag = drag.reshape(slots, 3, lanes)
    velocity = bubble_velocity.reshape(slots, 3, lanes)
    gas_rows = gas.reshape(3 * tile.wx * tile.wy, tile.nz)
    per_x, per_y = tile.wx // REC, tile.wy // REC
    bind = functools.partial
    macs = tile.rows * 3 * tile.nz * 3 * 2 * lanes

    xsend, own = call(
        bind(pack_kernel, tile, slots),
        [(2, 3 * CAP + 3 * per_y, REC, lanes), (2, CAP, REC, lanes)],
        [codes, cells, offsets, drag, velocity, gas_rows],
        [SMEM] + [VMEM] * 5,
        scratch=[pltpu.SMEM((9,), jnp.int32)],
        name="pack",
    )
    xrecv = exchange_x(xsend, "tx", count_x)
    ty_shape = (3 * CAP + 3 * per_x + 1, REC, lanes)
    send_a, send_b = call(
        bind(join_kernel, tile, "ty", count_y), [ty_shape] * 2, [xrecv, own, gas_rows], name="join"
    )
    recv_a, recv_b = exchange_y(send_a, send_b, "ty", count_y)
    (acc,) = call(
        bind(own_kernel, tile, slots),
        [(tile.rows, 3 * tile.nz)],
        [codes, cells, offsets, drag],
        [SMEM] + [VMEM] * 3,
        cost=(macs * slots, slots * lanes * 40),
        name="deposit_own",
    )
    edge_shape = (tile.edge_rows, tile.nz)
    acc, arrivals, edge_a, edge_b = call(
        bind(arrive_kernel, tile, "ty", count_y),
        [acc.shape, (8 * CAP, REC, lanes), edge_shape, edge_shape],
        [recv_a, recv_b, xrecv, acc],
        cost=(macs * 8 * CAP, 8 * CAP * lanes * 40),
        name="deposit_arrivals",
    )
    got_a, got_b = exchange_y(edge_a, edge_b, "ty", count_y)
    mid, beyond, xedge = call(
        bind(widen_kernel, tile, "ty", count_y),
        [
            (3, tile.yw, tile.wx, tile.nz),
            (3, 2, tile.yp, tile.nz),
            (2, 3 * tile.yw + 3 * (tile.yp // SUB), SUB, tile.nz),
        ],
        [acc, got_a, got_b],
        name="widen",
    )
    xgot = exchange_x(xedge, "tx", count_x)
    depth = round_up(3 * tile.rows, 128)
    wide = (3, tile.yw, tile.wx + 2 * SUB, tile.nz)
    gas_new, slip = call(
        bind(finish_kernel, tile, "ty", count_y, slots),
        [gas_rows.shape, (slots + 8 * CAP, 3, lanes)],
        [codes, cells, offsets, velocity, gas_rows, xrecv, recv_a, recv_b, arrivals, mid, beyond, xgot],
        [SMEM] + [VMEM] * 11,
        scratch=[
            pltpu.VMEM(wide, jnp.float32),
            pltpu.VMEM(wide, jnp.float32),
            pltpu.VMEM(wide, jnp.float32),
            pltpu.VMEM((3 * tile.nz, depth), jnp.bfloat16),
            pltpu.VMEM((3, tile.rows, tile.nz), jnp.float32),
        ],
        cost=(macs * (slots + 8 * CAP), (slots + 8 * CAP) * lanes * 40),
        name="finish",
    )
    return gas_new.reshape(gas.shape), slip.reshape(1, 1, slots + 8 * CAP, 3, lanes)


def solution(mesh):
    return jax.shard_map(
        functools.partial(on_device, mesh.shape["tx"], mesh.shape["ty"]),
        mesh=mesh,
        in_specs=(
            P("tx", "ty", None, None),
            P("tx", "ty", None, None),
            P("tx", "ty", None, None, None),
            P("tx", "ty", None, None, None),
            P("tx", "ty", None, None, None),
            P(None, "tx", "ty", None),
        ),
        out_specs=(P(None, "tx", "ty", None), P("tx", "ty", None, None, None)),
        check_vma=False,
    )
```

```python
import functools

import jax
import jax.numpy as jnp
from jax import lax
from jax.experimental import pallas as pl
from jax.experimental.pallas import tpu as pltpu
from jax.sharding import PartitionSpec as P

SWEEPS = 4
CAP = 2
DIFFUSE = 1.0
STEP_SIZE = 2.0

REC = 16
STAY = 4
REACH = SWEEPS + 1
EDGE = REACH + 1
SUB = 8
VMEM = pl.BlockSpec(memory_space=pltpu.VMEM)
SMEM = pl.BlockSpec(memory_space=pltpu.SMEM)
HBM = pl.BlockSpec(memory_space=pltpu.HBM)
ANY = pl.BlockSpec(memory_space=pl.ANY)
LIMIT = 24 * 1024 * 1024
COLS = 16


def round_up(count, unit):
    return -(-count // unit) * unit


def call(body, outs, args, specs=None, scratch=(), cost=(0, 0), name=None, results=False):
    specs = specs or [VMEM] * len(args)
    kind = jax.ShapeDtypeStruct if results else pltpu.VMEM
    return pl.pallas_call(
        body,
        out_shape=[
            kind(*out) if isinstance(out[0], tuple) else kind(out, jnp.float32) for out in outs
        ],
        in_specs=specs,
        out_specs=[VMEM] * len(outs),
        scratch_shapes=list(scratch),
        compiler_params=pltpu.CompilerParams(vmem_limit_bytes=LIMIT),
        cost_estimate=pl.CostEstimate(flops=cost[0], bytes_accessed=cost[1], transcendentals=0),
        name=name,
    )(
        *[
            arg if spec in (SMEM, ANY) else pltpu.with_memory_space_constraint(arg, spec.memory_space)
            for arg, spec in zip(args, specs)
        ]
    )


def split_by(value, size):
    if size & (size - 1) == 0:
        return value >> (size.bit_length() - 1), value & (size - 1)
    return value // size, value % size


class Tile:
    def __init__(self, wx, wy, nz):
        self.wx, self.wy, self.nz = wx, wy, nz
        self.ye = wy + 2
        self.hp = round_up(self.ye, SUB)
        self.main = self.ye * wx
        self.rows = self.main + 2 * self.hp
        self.yw = wy + 2 * REACH
        self.yp = round_up(self.yw, SUB)
        self.edge_main = EDGE * wx
        self.edge_rows = round_up(3 * (self.edge_main + 2 * EDGE), SUB)

    def decode(self, cell):
        cx, rest = split_by(cell, self.wy * self.nz)
        cy, cz = split_by(rest, self.nz)
        return cx, cy, cz

    def prepare(self, first, cell, sixteenths, fields, columns, force=None):
        count = cell.shape[0]
        cx, cy, cz = self.decode(cell)
        rows = slice(first, first + count)
        fields[0, rows] = cx.astype(jnp.float32)
        fields[1, rows] = cy.astype(jnp.float32)
        for axis in range(2):
            for i, weight in enumerate(tsc_weights(sixteenths[axis])):
                fields[2 + 3 * axis + i, rows] = weight
        below = jnp.where(cz == 0, self.nz - 1, cz - 1).astype(jnp.float32)
        above = jnp.where(cz == self.nz - 1, 0, cz + 1).astype(jnp.float32)
        values = [below, cz.astype(jnp.float32), above, *tsc_weights(sixteenths[2])]
        if force is not None:
            values += force
        for i, value in enumerate(values):
            columns[pl.ds(first * COLS + i, count, stride=COLS), :] = value

    def vertical(self, columns, slot):
        start = pl.multiple_of(slot * COLS, COLS)
        rows = [columns[pl.ds(start, COLS), :][j : j + 1] for j in range(9)]
        iz = lax.broadcasted_iota(jnp.int32, (self.nz, rows[0].shape[1]), 0).astype(jnp.float32)
        tz = jnp.where(iz == rows[2], rows[5], 0.0)
        tz = jnp.where(iz == rows[1], rows[4], tz)
        return jnp.where(iz == rows[0], rows[3], tz), rows[6:9]

    def planar(self, fields, slot):
        lanes = fields.shape[2]
        cx, cy, *weights = [fields[i, pl.ds(slot, 1), :] for i in range(8)]
        ix = lax.broadcasted_iota(jnp.int32, (self.wx, lanes), 0).astype(jnp.float32)
        tx = jnp.where(ix == cx + 1.0, weights[2], 0.0)
        tx = jnp.where(ix == cx, weights[1], tx)
        tx = jnp.where(ix == cx - 1.0, weights[0], tx)
        iy = lax.broadcasted_iota(jnp.int32, (self.hp, lanes), 0).astype(jnp.float32)
        ty = jnp.where(iy == cy + 2.0, weights[5], 0.0)
        ty = jnp.where(iy == cy + 1.0, weights[4], ty)
        ty = jnp.where(iy == cy, weights[3], ty)
        beyond_low = jnp.where(cx == 0.0, weights[0], 0.0)
        beyond_high = jnp.where(cx == self.wx - 1.0, weights[2], 0.0)
        parts = [tx * ty[j : j + 1] for j in range(self.ye)]
        return parts + [jnp.concatenate([ty * beyond_low, ty * beyond_high], axis=0)]


def tsc_weights(sixteenths):
    fraction = (sixteenths + 0.5) * (1.0 / 16.0) - 0.5
    low = 0.5 - fraction
    high = 0.5 + fraction
    return 0.5 * low * low, 0.75 - fraction * fraction, 0.5 * high * high


def halves(value):
    top = value.astype(jnp.bfloat16)
    return top, (value - top.astype(jnp.float32)).astype(jnp.bfloat16)


def put_planar(tile, fields, slot, ref, top_at, low_at):
    row = 0
    for part in tile.planar(fields, slot):
        top, low = halves(part)
        count = part.shape[0]
        for (slab, first), value in ((top_at, top), (low_at, low)):
            ref[slab, first + row : first + row + count] = value
        row += count


def pipeline(steps, build, use):
    build(0, 0)
    assert steps % 2 == 0

    def pair(i, carry):
        use(0, 2 * i)
        build(1, 2 * i + 1)
        use(1, 2 * i + 1)
        build(0, 2 * i + 2)
        return carry

    lax.fori_loop(0, steps // 2 - 1, pair, 0, unroll=True)
    use(0, steps - 2)
    build(1, steps - 1)
    use(1, steps - 1)


def deposit(tile, slots, fields, columns, acc, left, right):
    def build(buffer, step):
        for i in range(2):
            slot = step * 2 + i
            put_planar(tile, fields, slot, left[buffer], (i, 0), (2 + i, 0))
            tz, force = tile.vertical(columns, slot)
            for k in range(3):
                top, low = halves(tz * force[k])
                right[buffer][i, k * tile.nz : (k + 1) * tile.nz] = top
                right[buffer][2 + i, k * tile.nz : (k + 1) * tile.nz] = low

    def use(buffer, step):
        a = [left[buffer][i] for i in range(4)]
        b = [right[buffer][i] for i in range(4)]
        both = [jnp.concatenate([a[i], a[2 + i]], axis=0) for i in range(2)]
        nt = (((1,), (1,)), ((), ()))
        first = lax.dot_general(
            jnp.concatenate(both, axis=1),
            jnp.concatenate(b[:2], axis=1),
            nt,
            preferred_element_type=jnp.float32,
        )
        second = lax.dot_general(
            jnp.concatenate(a[:2], axis=1),
            jnp.concatenate(b[2:], axis=1),
            nt,
            preferred_element_type=jnp.float32,
        )
        acc[...] += first[: tile.rows] + first[tile.rows :] + second

    pipeline(slots // 2, build, use)


def ty_roles(axis, count):
    if count % 2:
        return True, False
    even = lax.axis_index(axis) % 2 == 0
    return even, even


def if_(cond, then, other):
    if isinstance(cond, bool):
        (then if cond else other)()
        return
    pl.when(cond)(then)
    pl.when(jnp.logical_not(cond))(other)


def pack_kernel(
    tile, slots, codes, cells_in, offsets_in, drag_in, velocity_in, gas_in,
    xsend, own, stays, cells, offsets, drag, velocity, gas, counts, sems,
):
    sources = (cells_in, offsets_in, drag_in, velocity_in, gas_in)
    targets = (cells, offsets, drag, velocity, gas)
    copies = [
        pltpu.make_async_copy(source, target, sems.at[i])
        for i, (source, target) in enumerate(zip(sources, targets))
    ]
    for copy in copies:
        copy.start()
    xsend[:, : 3 * CAP] = jnp.zeros((2, 3 * CAP, REC, 128), jnp.float32)
    own[...] = jnp.zeros(own.shape, jnp.float32)
    for code in range(9):
        counts[code] = 0
    for copy in copies:
        copy.wait()
    per = tile.wy // REC
    for k in range(3):
        for side, x in ((0, 0), (1, tile.wx - 1)):
            for part in range(per):
                start = (k * tile.wx + x) * tile.wy + part * REC
                xsend[side, 3 * CAP + k * per + part] = gas[start : start + REC]

    def visit(slot, carry):
        code = codes[slot]
        here = pl.ds(slot, 1)
        stays[here] = jnp.full((1, 128), (code == STAY).astype(jnp.float32), jnp.float32)

        @pl.when(code != STAY)
        def _():
            rank = jnp.minimum(counts[code], CAP - 1)
            counts[code] = rank + 1

            def put(ref, side, place):
                for k in range(3):
                    ref[side, place, k : k + 1] = drag[k, here]
                    ref[side, place, 3 + k : 4 + k] = velocity[k, here]
                    ref[side, place, 7 + k : 8 + k] = offsets[k, here].astype(jnp.float32)
                ref[side, place, 6:7] = cells[here].astype(jnp.float32)
                ref[side, place, 10:11] = jnp.ones((1, 128), jnp.float32)

            step_x, step_y = code // 3, code % 3
            pl.when(step_x == 1)(lambda: put(own, step_y // 2, rank))
            pl.when(step_x != 1)(lambda: put(xsend, step_x // 2, step_y * CAP + rank))

        return carry

    lax.fori_loop(0, slots, visit, 0)


def join_kernel(tile, axis, count, xrecv, own, gas, send_a, send_b):
    a_high, _ = ty_roles(axis, count)
    per_x, per_y = tile.wx // REC, tile.wy // REC

    def fill(ref, high):
        step = 2 * CAP * int(high)
        y = tile.wy - 1 if high else 0
        for s in range(CAP):
            ref[s] = xrecv[1, step + s]
            ref[CAP + s] = own[int(high), s]
            ref[2 * CAP + s] = xrecv[0, step + s]
        for k in range(3):
            for part in range(per_x):
                start = (k * tile.wx + part * REC) * tile.wy + y
                ref[3 * CAP + k * per_x + part] = gas[pl.ds(start, REC, stride=tile.wy), :]
            place = 3 * CAP + k * per_y + y // REC
            corner = 3 * CAP + 3 * per_x
            ref[corner, 2 * k : 2 * k + 1] = xrecv[1, place, y % REC : y % REC + 1]
            ref[corner, 2 * k + 1 : 2 * k + 2] = xrecv[0, place, y % REC : y % REC + 1]

    def even():
        fill(send_a, True)
        fill(send_b, False)

    def odd():
        fill(send_a, False)
        fill(send_b, True)

    for ref in (send_a, send_b):
        ref[3 * CAP + 3 * per_x] = jnp.zeros((REC, 128), jnp.float32)
    if_(a_high, even, odd)


def table_scratch(tile, slots):
    left, right = (4, tile.rows, 128), (4, 3 * tile.nz, 128)
    return [
        pltpu.VMEM((8, slots, 128), jnp.float32),
        pltpu.VMEM((slots * COLS, 128), jnp.float32),
        *[pltpu.VMEM(shape, jnp.bfloat16) for shape in (left, left, right, right)],
    ]


def own_kernel(tile, slots, cells, offsets, drag, stays, acc, fields, columns, la, lb, ra, rb):
    acc[...] = jnp.zeros(acc.shape, jnp.float32)
    sixteenths = [offsets[k].astype(jnp.float32) for k in range(3)]
    force = [drag[k] * stays[...] for k in range(3)]
    columns[...] = jnp.zeros(columns.shape, jnp.float32)
    tile.prepare(0, cells[...], sixteenths, fields, columns, force)
    deposit(tile, slots, fields, columns, acc, (la, lb), (ra, rb))


def record_row(records, row, count):
    return records[pl.ds(row, count, stride=REC), :]


ARRIVAL_LOW, ARRIVAL_HIGH = (0, 3, 5), (2, 4, 7)


def arrive_kernel(
    tile, axis, count, recv_a, recv_b, xrecv, acc_in, acc, arrivals, send_a, send_b,
    fields, columns, la, lb, ra, rb,
):
    a_high, a_from_high = ty_roles(axis, count)
    for s in range(CAP):
        arrivals[(1 * CAP + s) * REC : (1 * CAP + s + 1) * REC] = xrecv[1, CAP + s]
        arrivals[(6 * CAP + s) * REC : (6 * CAP + s + 1) * REC] = xrecv[0, CAP + s]

    def place(ref, order):
        for i, j in enumerate(order):
            for s in range(CAP):
                arrivals[(j * CAP + s) * REC : (j * CAP + s + 1) * REC] = ref[i * CAP + s]

    if_(
        a_from_high,
        lambda: (place(recv_a, ARRIVAL_HIGH), place(recv_b, ARRIVAL_LOW)) and None,
        lambda: (place(recv_a, ARRIVAL_LOW), place(recv_b, ARRIVAL_HIGH)) and None,
    )
    acc[...] = acc_in[...]

    blocks = 8 * CAP
    live = record_row(arrivals, 10, blocks)
    force = [record_row(arrivals, k, blocks) * live for k in range(3)]
    sixteenths = [record_row(arrivals, 7 + k, blocks) for k in range(3)]
    columns[...] = jnp.zeros(columns.shape, jnp.float32)
    cell = record_row(arrivals, 6, blocks).astype(jnp.int32)
    tile.prepare(0, cell, sixteenths, fields, columns, force)
    deposit(tile, blocks, fields, columns, acc, (la, lb), (ra, rb))

    def edge(ref, high):
        first = tile.ye - EDGE if high else 0
        tail = 3 * tile.edge_main
        for k in range(3):
            lanes = slice(k * tile.nz, (k + 1) * tile.nz)
            ref[k * tile.edge_main : (k + 1) * tile.edge_main] = acc[
                first * tile.wx : (first + EDGE) * tile.wx, lanes
            ]
            for h in range(2):
                start = tile.main + h * tile.hp + first
                row = tail + (2 * k + h) * EDGE
                ref[row : row + EDGE] = acc[start : start + EDGE, lanes]

    def even():
        edge(send_a, True)
        edge(send_b, False)

    def odd():
        edge(send_a, False)
        edge(send_b, True)

    for ref in (send_a, send_b):
        last = tile.edge_rows - SUB
        ref[last:] = jnp.zeros((SUB, tile.nz), jnp.float32)
    if_(a_high, even, odd)


def widen_kernel(tile, axis, count, acc, recv_a, recv_b, verticals, mid, beyond, xsend):
    _, a_from_high = ty_roles(axis, count)
    own = slice(REACH - 1, REACH - 1 + tile.ye)
    for k in range(3):
        lanes = slice(k * tile.nz, (k + 1) * tile.nz)
        zero = jnp.zeros((REACH - 1, tile.wx, tile.nz), jnp.float32)
        mid[k, : REACH - 1] = zero
        mid[k, REACH - 1 + tile.ye :] = zero
        mid[k, own] = acc[: tile.main, lanes].reshape(tile.ye, tile.wx, tile.nz)
        for h in range(2):
            start = tile.main + h * tile.hp
            beyond[k, h] = jnp.zeros((tile.yp, tile.nz), jnp.float32)
            beyond[k, h, own] = acc[start : start + tile.ye, lanes]

    def add(ref, high):
        first = tile.yw - EDGE if high else 0
        tail = 3 * tile.edge_main
        for k in range(3):
            rows = ref[k * tile.edge_main : (k + 1) * tile.edge_main]
            mid[k, first : first + EDGE] += rows.reshape(EDGE, tile.wx, tile.nz)
            for h in range(2):
                row = tail + (2 * k + h) * EDGE
                beyond[k, h, first : first + EDGE] += ref[row : row + EDGE]

    if_(
        a_from_high,
        lambda: (add(recv_a, True), add(recv_b, False)) and None,
        lambda: (add(recv_a, False), add(recv_b, True)) and None,
    )
    tail = 3 * tile.yw
    for k in range(3):
        for side, first in ((0, 0), (1, tile.wx - SUB)):
            for y in range(tile.yw):
                xsend[side, k * tile.yw + y] = mid[k, y, first : first + SUB]
            for part in range(tile.yp // SUB):
                xsend[side, tail + k * (tile.yp // SUB) + part] = beyond[
                    k, side, part * SUB : (part + 1) * SUB
                ]


def tables_kernel(tile, slots, cells, offsets, arrivals, tables, verticals, fields, columns):
    blocks = 8 * CAP
    tile.prepare(0, cells[...], [offsets[k].astype(jnp.float32) for k in range(3)], fields, columns)
    sixteenths = [record_row(arrivals, 7 + k, blocks) for k in range(3)]
    cell = record_row(arrivals, 6, blocks).astype(jnp.int32)
    tile.prepare(slots, cell, sixteenths, fields, columns)

    def build(pair, carry):
        for i in range(2):
            slot = pair * 2 + i
            put_planar(tile, fields, slot, tables, (slot, 0), (slot, tile.rows))
            verticals[slot], _ = tile.vertical(columns, slot)
        return carry

    lax.fori_loop(0, (slots + blocks) // 2, build, 0)


def finish_kernel(
    tile, axis, count, slots, stays, velocity, gas, xgas, ygas_a, ygas_b, arrivals,
    tables, verticals, mid, beyond, xrecv, gas_new, slip, src, ping, pong, field, stack,
):
    _, a_from_high = ty_roles(axis, count)
    zero = SUB + SWEEPS
    after = zero + tile.wx
    swept = tile.wx + 2 * SWEEPS
    tail = 3 * tile.yw
    parts = tile.yp // SUB
    for k in range(3):
        for y in range(tile.yw):
            place = tail + k * parts + y // SUB
            row = y % SUB
            src[k, y, zero - SUB : zero] = xrecv[1, k * tile.yw + y]
            src[k, y, zero:after] = mid[k, y]
            src[k, y, after : after + SUB] = xrecv[0, k * tile.yw + y]
            src[k, y, zero - 1 : zero] += beyond[k, 0, y : y + 1]
            src[k, y, after : after + 1] += beyond[k, 1, y : y + 1]
            src[k, y, zero : zero + 1] += xrecv[1, place, row : row + 1]
            src[k, y, after - 1 : after] += xrecv[0, place, row : row + 1]

    def sweep(old, new, margin):
        def row(y, carry):
            for k in range(3):
                here = old[k, y, SUB : SUB + swept]
                around = old[k, y - 1, SUB : SUB + swept] + old[k, y + 1, SUB : SUB + swept]
                around = around + old[k, y, SUB - 1 : SUB - 1 + swept]
                around = around + old[k, y, SUB + 1 : SUB + 1 + swept]
                around = around + pltpu.roll(here, 1, 1) + pltpu.roll(here, tile.nz - 1, 1)
                total = src[k, y, SUB : SUB + swept] + DIFFUSE * around
                new[k, y, SUB : SUB + swept] = total * (1.0 / (1.0 + 6.0 * DIFFUSE))
            return carry

        rows = tile.yw - 2 * margin
        lax.fori_loop(margin, tile.yw - margin, row, 0, unroll=rows // 2)

    buffers = [src, ping, pong, ping, pong]
    for index in range(SWEEPS):
        sweep(buffers[index], buffers[index + 1], index + 1)
    filtered = buffers[SWEEPS]

    per_x, per_y = tile.wx // REC, tile.wy // REC

    def take_edges(ref, high):
        y = tile.ye - 1 if high else 0
        for k in range(3):
            for part in range(per_x):
                row = y * tile.wx + part * REC
                stack[k, row : row + REC] = ref[3 * CAP + k * per_x + part]
            corner = 3 * CAP + 3 * per_x
            for h in range(2):
                row = tile.main + h * tile.hp + y
                stack[k, row : row + 1] = ref[corner, 2 * k + h : 2 * k + h + 1]

    for k in range(3):
        for h in range(2):
            start = tile.main + h * tile.hp
            stack[k, start : start + tile.hp] = jnp.zeros((tile.hp, tile.nz), jnp.float32)
            for part in range(per_y):
                row = start + 1 + part * REC
                stack[k, row : row + REC] = xgas[1 - h, 3 * CAP + k * per_y + part]
        for y in range(tile.wy):
            stack[k, (y + 1) * tile.wx : (y + 2) * tile.wx] = gas[
                pl.ds(k * tile.wx * tile.wy + y, tile.wx, stride=tile.wy), :
            ]
    if_(
        a_from_high,
        lambda: (take_edges(ygas_a, True), take_edges(ygas_b, False)) and None,
        lambda: (take_edges(ygas_a, False), take_edges(ygas_b, True)) and None,
    )
    depth = field.shape[0] * 128
    for k in range(3):
        for y in range(tile.ye):
            rows = slice(y * tile.wx, (y + 1) * tile.wx)
            updated = stack[k, rows] + STEP_SIZE * filtered[k, y + REACH - 1, zero:after]
            stack[k, rows] = updated
            if 1 <= y <= tile.wy:
                gas_new[pl.ds(k * tile.wx * tile.wy + y - 1, tile.wx, stride=tile.wy), :] = updated
            for h, x in ((0, zero - 1), (1, after)):
                row = tile.main + h * tile.hp + y
                stack[k, row : row + 1] += STEP_SIZE * filtered[k, y + REACH - 1, x : x + 1]
        whole = stack[k]
        top = whole.astype(jnp.bfloat16).astype(jnp.float32)
        pad = jnp.zeros((depth - 3 * tile.rows, tile.nz), jnp.float32)
        both = jnp.concatenate([top, top, whole - top, pad], axis=0)
        turned = both.T.astype(jnp.bfloat16)
        for i in range(depth // 128):
            field[i, k * tile.nz : (k + 1) * tile.nz] = turned[:, i * 128 : (i + 1) * 128]

    blocks = 8 * CAP
    total = slots + blocks

    def sample(pair, carry):
        pad = jnp.zeros((depth - 3 * tile.rows, 128), jnp.bfloat16)
        slabs = [tables[pair * 2 + i] for i in range(2)]
        slabs = [jnp.concatenate([slab, slab[: tile.rows], pad], axis=0) for slab in slabs]
        column = jnp.dot(
            jnp.concatenate([field[i] for i in range(depth // 128)], axis=1),
            jnp.concatenate(slabs, axis=1),
            preferred_element_type=jnp.float32,
        )
        for i in range(2):
            vertical = verticals[pair * 2 + i]
            for k in range(3):
                part = column[k * tile.nz : (k + 1) * tile.nz, i * 128 : (i + 1) * 128]
                value = jnp.sum(part * vertical, axis=0, keepdims=True)
                slip[k, pl.ds(pair * 2 + i, 1)] = value
        return carry

    lax.fori_loop(0, total // 2, sample, 0, unroll=8)
    live = record_row(arrivals, 10, blocks)
    for k in range(3):
        slip[k, :slots] = (slip[k, :slots] - velocity[k]) * stays[...]
        slip[k, slots:] = (slip[k, slots:] - record_row(arrivals, 3 + k, blocks)) * live


def exchange_x(buffer, axis, count):
    forward = [(i, (i + 1) % count) for i in range(count)]
    backward = [(target, source) for source, target in forward]
    if count == 2:
        return lax.ppermute(buffer, axis, forward)
    return jnp.stack(
        [lax.ppermute(buffer[0], axis, backward), lax.ppermute(buffer[1], axis, forward)]
    )


def exchange_y(send_a, send_b, axis, count):
    if count % 2:
        perm_a = [(i, (i + 1) % count) for i in range(count)]
        perm_b = [(target, source) for source, target in perm_a]
    else:
        perm_a = [(i, i ^ 1) for i in range(count)]
        perm_b = [(i, (i + 1) % count if i % 2 else (i - 1) % count) for i in range(count)]
    return lax.ppermute(send_a, axis, perm_a), lax.ppermute(send_b, axis, perm_b)


def on_device(count_x, count_y, handoff, cells, offsets, drag, bubble_velocity, gas):
    tile = Tile(gas.shape[1], gas.shape[2], gas.shape[3])
    slots, lanes = cells.shape[2], cells.shape[3]
    codes = handoff.reshape(slots)
    cells = cells.reshape(slots, lanes)
    offsets = offsets.reshape(slots, 3, lanes).transpose(1, 0, 2)
    drag = drag.reshape(slots, 3, lanes).transpose(1, 0, 2)
    velocity = bubble_velocity.reshape(slots, 3, lanes).transpose(1, 0, 2)
    gas_rows = gas.reshape(3 * tile.wx * tile.wy, tile.nz)
    per_x, per_y = tile.wx // REC, tile.wy // REC
    bind = functools.partial
    macs = tile.rows * 3 * tile.nz * 3 * 2 * lanes

    inputs = [cells, offsets, drag, velocity, gas_rows]
    xsend, own, stays, cells, offsets, drag, velocity, gas_rows = call(
        bind(pack_kernel, tile, slots),
        [(2, 3 * CAP + 3 * per_y, REC, lanes), (2, CAP, REC, lanes), (slots, lanes)]
        + [(value.shape, value.dtype) for value in inputs],
        [codes, *inputs],
        [SMEM] + [HBM] * 5,
        scratch=[pltpu.SMEM((9,), jnp.int32), pltpu.SemaphoreType.DMA((5,))],
        name="pack",
    )
    xrecv = exchange_x(xsend, "tx", count_x)
    ty_shape = (3 * CAP + 3 * per_x + 1, REC, lanes)
    send_a, send_b = call(
        bind(join_kernel, tile, "ty", count_y), [ty_shape] * 2, [xrecv, own, gas_rows], name="join"
    )
    recv_a, recv_b = exchange_y(send_a, send_b, "ty", count_y)
    (acc,) = call(
        bind(own_kernel, tile, slots),
        [(tile.rows, 3 * tile.nz)],
        [cells, offsets, drag, stays],
        scratch=table_scratch(tile, slots),
        cost=(macs * slots, slots * lanes * 40),
        name="deposit_own",
    )
    edge_shape = (tile.edge_rows, tile.nz)
    blocks = 8 * CAP
    acc, arrivals, edge_a, edge_b = call(
        bind(arrive_kernel, tile, "ty", count_y),
        [acc.shape, (blocks * REC, lanes), edge_shape, edge_shape],
        [recv_a, recv_b, xrecv, acc],
        scratch=table_scratch(tile, blocks),
        cost=(macs * blocks, blocks * lanes * 40),
        name="deposit_arrivals",
    )
    got_a, got_b = exchange_y(edge_a, edge_b, "ty", count_y)
    total = slots + blocks
    tables, verticals = call(
        bind(tables_kernel, tile, slots),
        [((total, 2 * tile.rows, lanes), jnp.bfloat16), (total, tile.nz, lanes)],
        [cells, offsets, arrivals],
        scratch=[
            pltpu.VMEM((8, total, lanes), jnp.float32),
            pltpu.VMEM((total * COLS, lanes), jnp.float32),
        ],
        cost=(macs * total // 2, total * lanes * 40),
        name="tables",
    )
    mid, beyond, xedge = call(
        bind(widen_kernel, tile, "ty", count_y),
        [
            (3, tile.yw, tile.wx, tile.nz),
            (3, 2, tile.yp, tile.nz),
            (2, 3 * tile.yw + 3 * (tile.yp // SUB), SUB, tile.nz),
        ],
        [acc, got_a, got_b, verticals],
        [VMEM] * 3 + [ANY],
        name="widen",
    )
    xgot = exchange_x(xedge, "tx", count_x)
    depth = round_up(3 * tile.rows, 128)
    wide = (3, tile.yw, round_up(tile.wx + SUB + SWEEPS + SUB, SUB), tile.nz)
    gas_new, slip = call(
        bind(finish_kernel, tile, "ty", count_y, slots),
        [gas_rows.shape, (3, total, lanes)],
        [stays, velocity, gas_rows, xrecv, recv_a, recv_b, arrivals]
        + [tables, verticals, mid, beyond, xgot],
        scratch=[
            *[pltpu.VMEM(wide, jnp.float32)] * 3,
            pltpu.VMEM((depth // 128, 3 * tile.nz, 128), jnp.bfloat16),
            pltpu.VMEM((3, tile.rows, tile.nz), jnp.float32),
        ],
        cost=(macs * total, total * lanes * 40),
        name="finish",
        results=True,
    )
    return gas_new.reshape(gas.shape), slip.transpose(1, 0, 2).reshape(1, 1, total, 3, lanes)


def solution(mesh):
    return jax.shard_map(
        functools.partial(on_device, mesh.shape["tx"], mesh.shape["ty"]),
        mesh=mesh,
        in_specs=(
            P("tx", "ty", None, None),
            P("tx", "ty", None, None),
            P("tx", "ty", None, None, None),
            P("tx", "ty", None, None, None),
            P("tx", "ty", None, None, None),
            P(None, "tx", "ty", None),
        ),
        out_specs=(P(None, "tx", "ty", None), P("tx", "ty", None, None, None)),
        check_vma=False,
    )
```

```python
import functools

import jax
import jax.numpy as jnp
from jax import lax
from jax.experimental import pallas as pl
from jax.experimental.pallas import tpu as pltpu
from jax.sharding import PartitionSpec as P

SWEEPS = 4
CAP = 2
DIFFUSE = 1.0
STEP_SIZE = 2.0

REC = 16
STAY = 4
REACH = SWEEPS + 1
EDGE = REACH + 1
SUB = 8
VMEM = pl.BlockSpec(memory_space=pltpu.VMEM)
SMEM = pl.BlockSpec(memory_space=pltpu.SMEM)
HBM = pl.BlockSpec(memory_space=pltpu.HBM)
ANY = pl.BlockSpec(memory_space=pl.ANY)
F8 = jnp.float8_e4m3fn
PEAK = 400.0
PLANAR_SCALE = 512.0
TINY = 1e-20
COARSE = 256
LIMIT = 24 * 1024 * 1024
COLS = 16


def round_up(count, unit):
    return -(-count // unit) * unit


def call(
    body, outs, args, specs=None, out_specs=None, scratch=(), cost=(0, 0), name=None, results=False
):
    specs = specs or [VMEM] * len(args)
    kind = jax.ShapeDtypeStruct if results else pltpu.VMEM
    return pl.pallas_call(
        body,
        out_shape=[
            kind(*out) if isinstance(out[0], tuple) else kind(out, jnp.float32) for out in outs
        ],
        in_specs=specs,
        out_specs=out_specs or [VMEM] * len(outs),
        scratch_shapes=list(scratch),
        compiler_params=pltpu.CompilerParams(vmem_limit_bytes=LIMIT),
        cost_estimate=pl.CostEstimate(flops=cost[0], bytes_accessed=cost[1], transcendentals=0),
        name=name,
    )(
        *[
            arg if spec in (SMEM, ANY) else pltpu.with_memory_space_constraint(arg, spec.memory_space)
            for arg, spec in zip(args, specs)
        ]
    )


def split_by(value, size):
    if size & (size - 1) == 0:
        return value >> (size.bit_length() - 1), value & (size - 1)
    return value // size, value % size


class Tile:
    def __init__(self, wx, wy, nz):
        self.wx, self.wy, self.nz = wx, wy, nz
        self.ye = wy + 2
        self.hp = round_up(self.ye, SUB)
        self.main = self.ye * wx
        self.rows = self.main + 2 * self.hp
        self.rows8 = round_up(self.rows, 4 * SUB)
        self.yw = wy + 2 * REACH
        self.yp = round_up(self.yw, SUB)
        self.edge_main = EDGE * wx
        self.edge_rows = round_up(3 * (self.edge_main + 2 * EDGE), SUB)

    def decode(self, cell):
        cx, rest = split_by(cell, self.wy * self.nz)
        cy, cz = split_by(rest, self.nz)
        return cx, cy, cz

    def prepare(self, first, cell, sixteenths, fields, columns, force=None):
        count = cell.shape[0]
        cx, cy, cz = self.decode(cell)
        rows = slice(first, first + count)
        fields[0, rows] = cx.astype(jnp.float32)
        fields[1, rows] = cy.astype(jnp.float32)
        for axis in range(2):
            scale = 1.0 if axis else PLANAR_SCALE
            for i, weight in enumerate(tsc_weights(sixteenths[axis])):
                fields[2 + 3 * axis + i, rows] = weight * scale
        below = jnp.where(cz == 0, self.nz - 1, cz - 1).astype(jnp.float32)
        above = jnp.where(cz == self.nz - 1, 0, cz + 1).astype(jnp.float32)
        values = [below, cz.astype(jnp.float32), above, *tsc_weights(sixteenths[2])]
        if force is not None:
            values += force
        for i, value in enumerate(values):
            columns[pl.ds(first * COLS + i, count, stride=COLS), :] = value

    def vertical(self, columns, slot):
        start = pl.multiple_of(slot * COLS, COLS)
        rows = [columns[pl.ds(start, COLS), :][j : j + 1] for j in range(9)]
        iz = lax.broadcasted_iota(jnp.int32, (self.nz, rows[0].shape[1]), 0).astype(jnp.float32)
        tz = jnp.where(iz == rows[2], rows[5], 0.0)
        tz = jnp.where(iz == rows[1], rows[4], tz)
        return jnp.where(iz == rows[0], rows[3], tz), rows[6:9]

    def planar(self, fields, slot):
        lanes = fields.shape[2]
        cx, cy, *weights = [fields[i, pl.ds(slot, 1), :] for i in range(8)]
        ix = lax.broadcasted_iota(jnp.int32, (self.wx, lanes), 0).astype(jnp.float32)
        tx = jnp.where(ix == cx + 1.0, weights[2], 0.0)
        tx = jnp.where(ix == cx, weights[1], tx)
        tx = jnp.where(ix == cx - 1.0, weights[0], tx)
        iy = lax.broadcasted_iota(jnp.int32, (self.hp, lanes), 0).astype(jnp.float32)
        ty = jnp.where(iy == cy + 2.0, weights[5], 0.0)
        ty = jnp.where(iy == cy + 1.0, weights[4], ty)
        ty = jnp.where(iy == cy, weights[3], ty)
        beyond_low = jnp.where(cx == 0.0, weights[0], 0.0)
        beyond_high = jnp.where(cx == self.wx - 1.0, weights[2], 0.0)
        parts = [
            jnp.concatenate([tx * ty[j : j + 1], tx * ty[j + 1 : j + 2]], axis=0)
            for j in range(0, self.ye, 2)
        ]
        return parts + [jnp.concatenate([ty * beyond_low, ty * beyond_high], axis=0)]


def tsc_weights(sixteenths):
    fraction = (sixteenths + 0.5) * (1.0 / 16.0) - 0.5
    low = 0.5 - fraction
    high = 0.5 + fraction
    return 0.5 * low * low, 0.75 - fraction * fraction, 0.5 * high * high


def halves(value):
    top = value.astype(jnp.bfloat16)
    return top, value - top.astype(jnp.float32)


def scaled(values, bound):
    peak = functools.reduce(jnp.maximum, [jnp.abs(value) for value in values])
    peak = jnp.maximum(jnp.max(peak, keepdims=True), TINY)
    factor = (PEAK / bound) / peak
    return [value * factor for value in values], peak * (bound / PEAK)


def pipeline(steps, build, use):
    build(0, 0)
    assert steps % 2 == 0

    def pair(i, carry):
        use(0, 2 * i)
        build(1, 2 * i + 1)
        use(1, 2 * i + 1)
        build(0, 2 * i + 2)
        return carry

    lax.fori_loop(0, steps // 2 - 1, pair, 0, unroll=True)
    use(0, steps - 2)
    build(1, steps - 1)
    use(1, steps - 1)


def deposit(tile, slots, fields, columns, acc, cross, left, left8, right, right8):
    def build(buffer, step):
        for i in range(2):
            slot = step * 2 + i
            row = 0
            for part in tile.planar(fields, slot):
                top, low = halves(part)
                rows = slice(row, row + part.shape[0])
                left[buffer][i, rows] = top
                left8[buffer][i, rows] = part.astype(F8)
                left8[buffer][2 + i, rows] = low.astype(F8)
                row += part.shape[0]
            tz, force = tile.vertical(columns, slot)
            for k in range(3):
                value = (tz * force[k]).T
                top, low = halves(value)
                right[buffer][3 * i + k] = top
                right8[buffer][3 * i + k] = low.astype(F8)
                right8[buffer][3 * (2 + i) + k] = value.astype(F8)

    def use(buffer, step):
        def pieces(a_ref, b_ref, count):
            b = [jnp.concatenate([b_ref[3 * i + k] for k in range(3)], axis=1) for i in range(count)]
            return jnp.dot(
                jnp.concatenate([a_ref[i] for i in range(count)], axis=1),
                jnp.concatenate(b, axis=0),
                preferred_element_type=jnp.float32,
            )

        acc[...] += pieces(left[buffer], right[buffer], 2)
        cross[...] += pieces(left8[buffer], right8[buffer], 4)

    pipeline(slots // 2, build, use)


def ty_roles(axis, count):
    if count % 2:
        return True, False
    even = lax.axis_index(axis) % 2 == 0
    return even, even


def if_(cond, then, other):
    if isinstance(cond, bool):
        (then if cond else other)()
        return
    pl.when(cond)(then)
    pl.when(jnp.logical_not(cond))(other)


def pack_kernel(
    tile, axis, count, slots, codes_in, cells_in, offsets_in, drag_in, velocity_in, gas_in,
    send_a, send_b, own, stays, cells, offsets, drag, velocity, gas, codes, leaving, counts, sems,
):
    sources = (codes_in, cells_in, offsets_in, drag_in, velocity_in, gas_in)
    targets = (codes, cells, offsets, drag, velocity, gas)
    copies = [
        pltpu.make_async_copy(source, target, sems.at[i])
        for i, (source, target) in enumerate(zip(sources, targets))
    ]
    for copy in copies:
        copy.start()
    for ref in (send_a, send_b):
        ref[: 3 * CAP] = jnp.zeros((3 * CAP, REC, 128), jnp.float32)
    own[...] = jnp.zeros(own.shape, jnp.float32)
    for code in range(9):
        counts[code] = 0
    copies[0].wait()
    total = 0
    for slot in range(slots):
        code = codes[slot]
        stays[slot : slot + 1] = jnp.full((1, 128), (code == STAY).astype(jnp.float32), jnp.float32)
        leaving[total] = slot
        total = total + (code != STAY).astype(jnp.int32)
    for copy in copies[1:]:
        copy.wait()
    a_high, _ = ty_roles(axis, count)
    per = tile.wx // REC

    def edges(ref, high):
        y = tile.wy - 1 if high else 0
        for k in range(3):
            for part in range(per):
                start = (k * tile.wx + part * REC) * tile.wy + y
                ref[3 * CAP + k * per + part] = gas[pl.ds(start, REC, stride=tile.wy), :]

    def visit(index, carry):
        slot = leaving[index]
        code = codes[slot]
        rank = jnp.minimum(counts[code], CAP - 1)
        counts[code] = rank + 1
        here = pl.ds(slot, 1)

        def put(ref):
            for k in range(3):
                ref[k : k + 1] = drag[k, here]
                ref[3 + k : 4 + k] = velocity[k, here]
                ref[7 + k : 8 + k] = offsets[k, here].astype(jnp.float32)
            ref[6:7] = cells[here].astype(jnp.float32)
            ref[10:11] = jnp.ones((1, 128), jnp.float32)

        row = (code >= 3).astype(jnp.int32) + (code >= 6).astype(jnp.int32)
        column = code - 3 * row
        to_a = (column == 2) == a_high
        place = row * CAP + rank
        pl.when(column == 1)(lambda: put(own.at[(row >= 1).astype(jnp.int32), rank]))
        pl.when((column != 1) & to_a)(lambda: put(send_a.at[place]))
        pl.when((column != 1) & jnp.logical_not(to_a))(lambda: put(send_b.at[place]))
        return carry

    lax.fori_loop(0, total, visit, 0)
    if_(
        a_high,
        lambda: (edges(send_a, True), edges(send_b, False)) and None,
        lambda: (edges(send_a, False), edges(send_b, True)) and None,
    )


def join_kernel(tile, axis, count, recv_a, recv_b, own, gas, acc, xsend):
    _, a_from_high = ty_roles(axis, count)
    per_x, per_y = tile.wx // REC, tile.wy // REC
    corner = 3 * CAP + 3 * per_y
    for side, x in ((0, 0), (1, tile.wx - 1)):
        xsend[side, corner] = jnp.zeros((REC, 128), jnp.float32)
        for s in range(CAP):
            xsend[side, CAP + s] = own[side, s]
        for k in range(3):
            for part in range(per_y):
                start = (k * tile.wx + x) * tile.wy + part * REC
                xsend[side, 3 * CAP + k * per_y + part] = gas[start : start + REC]

    def forward(ref, high):
        first = 2 * CAP if high else 0
        for side, x in ((0, 0), (1, tile.wx - 1)):
            for s in range(CAP):
                xsend[side, first + s] = ref[2 * CAP * side + s]
            for k in range(3):
                place = 3 * CAP + k * per_x + x // REC
                row = 2 * k + int(high)
                xsend[side, corner, row : row + 1] = ref[place, x % REC : x % REC + 1]

    if_(
        a_from_high,
        lambda: (forward(recv_a, True), forward(recv_b, False)) and None,
        lambda: (forward(recv_a, False), forward(recv_b, True)) and None,
    )


def table_scratch(tile, slots):
    rows, turned = (tile.rows, 128), (128, tile.nz)
    return [
        pltpu.VMEM((8, slots, 128), jnp.float32),
        pltpu.VMEM((slots * COLS, 128), jnp.float32),
        *[pltpu.VMEM((2, *rows), jnp.bfloat16)] * 2,
        *[pltpu.VMEM((4, tile.rows8, 128), F8)] * 2,
        *[pltpu.VMEM((6, *turned), jnp.bfloat16)] * 2,
        *[pltpu.VMEM((12, *turned), F8)] * 2,
        pltpu.VMEM((tile.rows8, 3 * tile.nz), jnp.float32),
    ]


def deposit_blocks(tile, cell, sixteenths, force, acc, fields, columns, *buffers):
    acc[...] = jnp.zeros(acc.shape, jnp.float32)
    columns[...] = jnp.zeros(columns.shape, jnp.float32)
    force, factor = scaled(force, 0.75)
    tile.prepare(0, cell, sixteenths, fields, columns, force)
    cross = buffers[8]
    cross[...] = jnp.zeros(cross.shape, jnp.float32)
    pairs = [buffers[i : i + 2] for i in range(0, 8, 2)]
    for buffer in pairs[1]:
        buffer[:, tile.rows :] = jnp.zeros((4, tile.rows8 - tile.rows, 128), F8)
    deposit(tile, cell.shape[0], fields, columns, acc, cross, *pairs)
    acc[...] += cross[: tile.rows]
    return factor * (1.0 / PLANAR_SCALE)


def own_blocks(tile, first, count, cells, offsets, drag, stays, acc, *scratch):
    rows = slice(first, first + count)
    sixteenths = [offsets[k, rows].astype(jnp.float32) for k in range(3)]
    force = [drag[k, rows] * stays[rows] for k in range(3)]
    return deposit_blocks(tile, cells[rows], sixteenths, force, acc, *scratch)


def first_kernel(tile, count, cells, offsets, drag, stays, acc, *scratch):
    factor = own_blocks(tile, 0, count, cells, offsets, drag, stays, acc, *scratch)
    acc[...] = acc[...] * factor


def second_kernel(tile, first, count, cells, offsets, drag, stays, acc_in, xsend, acc, *scratch):
    factor = own_blocks(tile, first, count, cells, offsets, drag, stays, acc, *scratch)
    acc[...] = acc_in[...] + acc[...] * factor


def record_row(records, row, count):
    return records[pl.ds(row, count, stride=REC), :]


def arrive_kernel(
    tile, axis, count, recv_a, recv_b, xrecv, acc_in, acc, arrivals, send_a, send_b, *scratch
):
    a_high, a_from_high = ty_roles(axis, count)

    def place(j, record):
        arrivals[j * REC : (j + 1) * REC] = record

    for i in range(3 * CAP):
        place(i, xrecv[1, i])
        place(5 * CAP + i, xrecv[0, i])

    def middle(ref, j):
        for s in range(CAP):
            place(j * CAP + s, ref[CAP + s])

    if_(
        a_from_high,
        lambda: (middle(recv_a, 4), middle(recv_b, 3)) and None,
        lambda: (middle(recv_a, 3), middle(recv_b, 4)) and None,
    )
    blocks = 8 * CAP
    live = record_row(arrivals, 10, blocks)
    force = [record_row(arrivals, k, blocks) * live for k in range(3)]
    sixteenths = [record_row(arrivals, 7 + k, blocks) for k in range(3)]
    cell = record_row(arrivals, 6, blocks).astype(jnp.int32)
    factor = deposit_blocks(tile, cell, sixteenths, force, acc, *scratch)
    acc[...] = acc_in[...] + acc[...] * factor

    def edge(ref, high):
        first = tile.ye - EDGE if high else 0
        tail = 3 * tile.edge_main
        for k in range(3):
            lanes = slice(k * tile.nz, (k + 1) * tile.nz)
            ref[k * tile.edge_main : (k + 1) * tile.edge_main] = acc[
                first * tile.wx : (first + EDGE) * tile.wx, lanes
            ]
            for h in range(2):
                start = tile.main + h * tile.hp + first
                row = tail + (2 * k + h) * EDGE
                ref[row : row + EDGE] = acc[start : start + EDGE, lanes]

    def even():
        edge(send_a, True)
        edge(send_b, False)

    def odd():
        edge(send_a, False)
        edge(send_b, True)

    for ref in (send_a, send_b):
        last = tile.edge_rows - SUB
        ref[last:] = jnp.zeros((SUB, tile.nz), jnp.float32)
    if_(a_high, even, odd)


def widen_kernel(tile, axis, count, acc, recv_a, recv_b, verticals, mid, beyond, xsend):
    _, a_from_high = ty_roles(axis, count)
    own = slice(REACH - 1, REACH - 1 + tile.ye)
    for k in range(3):
        lanes = slice(k * tile.nz, (k + 1) * tile.nz)
        zero = jnp.zeros((REACH - 1, tile.wx, tile.nz), jnp.float32)
        mid[k, : REACH - 1] = zero
        mid[k, REACH - 1 + tile.ye :] = zero
        mid[k, own] = acc[: tile.main, lanes].reshape(tile.ye, tile.wx, tile.nz)
        for h in range(2):
            start = tile.main + h * tile.hp
            beyond[k, h] = jnp.zeros((tile.yp, tile.nz), jnp.float32)
            beyond[k, h, own] = acc[start : start + tile.ye, lanes]

    def add(ref, high):
        first = tile.yw - EDGE if high else 0
        tail = 3 * tile.edge_main
        for k in range(3):
            rows = ref[k * tile.edge_main : (k + 1) * tile.edge_main]
            mid[k, first : first + EDGE] += rows.reshape(EDGE, tile.wx, tile.nz)
            for h in range(2):
                row = tail + (2 * k + h) * EDGE
                beyond[k, h, first : first + EDGE] += ref[row : row + EDGE]

    if_(
        a_from_high,
        lambda: (add(recv_a, True), add(recv_b, False)) and None,
        lambda: (add(recv_a, False), add(recv_b, True)) and None,
    )
    for k in range(3):
        for y in range(tile.yw):
            row = (k * tile.yw + y) * EDGE
            xsend[0, row : row + 1] = beyond[k, 0, y : y + 1]
            xsend[0, row + 1 : row + EDGE] = mid[k, y, :REACH]
            xsend[1, row : row + REACH] = mid[k, y, tile.wx - REACH :]
            xsend[1, row + REACH : row + EDGE] = beyond[k, 1, y : y + 1]


def tables_kernel(
    tile, slots, cells, offsets, arrivals, tables, tables8, verticals, fields, columns
):
    blocks = 8 * CAP
    tile.prepare(0, cells[...], [offsets[k].astype(jnp.float32) for k in range(3)], fields, columns)
    sixteenths = [record_row(arrivals, 7 + k, blocks) for k in range(3)]
    cell = record_row(arrivals, 6, blocks).astype(jnp.int32)
    tile.prepare(slots, cell, sixteenths, fields, columns)

    def build(pair, carry):
        for i in range(2):
            slot = pair * 2 + i
            row = 0
            for part in tile.planar(fields, slot):
                top, low = halves(part)
                count = part.shape[0]
                tables[slot, row : row + count] = top
                if row < COARSE:
                    tables8[slot, row : row + count] = part.astype(F8)
                    tables8[slot, COARSE + row : COARSE + row + count] = low.astype(F8)
                else:
                    down = tile.rows - COARSE + row
                    tables[slot, down : down + count] = low.astype(jnp.bfloat16)
                row += count
            verticals[slot], _ = tile.vertical(columns, slot)
        return carry

    lax.fori_loop(0, (slots + blocks) // 2, build, 0)


def finish_kernel(
    tile, axis, count, slots, stays, velocity, gas, xgas, ygas_a, ygas_b, arrivals,
    tables, tables8, verticals, mid, beyond, xrecv, gas_out, slip,
    src, ping, pong, field, field8, stack, gas_new, sem,
):
    _, a_from_high = ty_roles(axis, count)
    zero = SUB + SWEEPS
    after = zero + tile.wx
    swept = tile.wx + 2 * SWEEPS
    for k in range(3):
        for y in range(tile.yw):
            row = (k * tile.yw + y) * EDGE
            src[k, y, zero - SUB : zero] = jnp.zeros((SUB, tile.nz), jnp.float32)
            src[k, y, zero:after] = mid[k, y]
            src[k, y, after : after + SUB] = jnp.zeros((SUB, tile.nz), jnp.float32)
            src[k, y, zero - REACH : zero] = xrecv[1, row : row + REACH]
            src[k, y, after : after + REACH] = xrecv[0, row + 1 : row + EDGE]
            src[k, y, zero - 1 : zero] += beyond[k, 0, y : y + 1]
            src[k, y, after : after + 1] += beyond[k, 1, y : y + 1]
            src[k, y, zero : zero + 1] += xrecv[1, row + REACH : row + EDGE]
            src[k, y, after - 1 : after] += xrecv[0, row : row + 1]

    def sweep(old, new, margin):
        def row(y, carry):
            for k in range(3):
                here = old[k, y, SUB : SUB + swept]
                around = old[k, y - 1, SUB : SUB + swept] + old[k, y + 1, SUB : SUB + swept]
                around = around + old[k, y, SUB - 1 : SUB - 1 + swept]
                around = around + old[k, y, SUB + 1 : SUB + 1 + swept]
                around = around + pltpu.roll(here, 1, 1) + pltpu.roll(here, tile.nz - 1, 1)
                total = src[k, y, SUB : SUB + swept] + DIFFUSE * around
                new[k, y, SUB : SUB + swept] = total * (1.0 / (1.0 + 6.0 * DIFFUSE))
            return carry

        rows = tile.yw - 2 * margin
        lax.fori_loop(margin, tile.yw - margin, row, 0, unroll=rows // 2)

    buffers = [src, ping, pong, ping, pong]
    for index in range(SWEEPS):
        sweep(buffers[index], buffers[index + 1], index + 1)
    filtered = buffers[SWEEPS]

    per_x, per_y = tile.wx // REC, tile.wy // REC

    def take_edges(ref, high):
        y = tile.ye - 1 if high else 0
        for k in range(3):
            for part in range(per_x):
                row = y * tile.wx + part * REC
                stack[k, row : row + REC] = ref[3 * CAP + k * per_x + part]
    for k in range(3):
        for h in range(2):
            start = tile.main + h * tile.hp
            stack[k, start : start + tile.hp] = jnp.zeros((tile.hp, tile.nz), jnp.float32)
            for part in range(per_y):
                row = start + 1 + part * REC
                stack[k, row : row + REC] = xgas[1 - h, 3 * CAP + k * per_y + part]
            corner = 3 * CAP + 3 * per_y
            stack[k, start : start + 1] = xgas[1 - h, corner, 2 * k : 2 * k + 1]
            last = start + tile.ye - 1
            stack[k, last : last + 1] = xgas[1 - h, corner, 2 * k + 1 : 2 * k + 2]
        for y in range(tile.wy):
            stack[k, (y + 1) * tile.wx : (y + 2) * tile.wx] = gas[
                pl.ds(k * tile.wx * tile.wy + y, tile.wx, stride=tile.wy), :
            ]
    if_(
        a_from_high,
        lambda: (take_edges(ygas_a, True), take_edges(ygas_b, False)) and None,
        lambda: (take_edges(ygas_a, False), take_edges(ygas_b, True)) and None,
    )
    for k in range(3):
        for y in range(tile.ye):
            rows = slice(y * tile.wx, (y + 1) * tile.wx)
            updated = stack[k, rows] + STEP_SIZE * filtered[k, y + REACH - 1, zero:after]
            stack[k, rows] = updated
            if 1 <= y <= tile.wy:
                gas_new[pl.ds(k * tile.wx * tile.wy + y - 1, tile.wx, stride=tile.wy), :] = updated
            for h, x in ((0, zero - 1), (1, after)):
                row = tile.main + h * tile.hp + y
                stack[k, row : row + 1] += STEP_SIZE * filtered[k, y + REACH - 1, x : x + 1]
    leave = pltpu.make_async_copy(gas_new, gas_out, sem)
    leave.start()
    blocks = 8 * CAP
    total = slots + blocks
    fine = tile.rows - COARSE
    pad_rows = round_up(3 * fine, 128) - 3 * fine
    values, factor = scaled([stack[k] for k in range(3)], 1.0)
    for k, value in enumerate(values):
        top = value.astype(jnp.bfloat16).astype(jnp.float32)
        low = value - top
        pad = jnp.zeros((pad_rows, tile.nz), jnp.float32)
        exact = jnp.concatenate([top, top[COARSE:], low[COARSE:], pad], axis=0).T
        cross = jnp.concatenate([low[:COARSE], value[:COARSE]], axis=0).T
        rows = slice(k * tile.nz, (k + 1) * tile.nz)
        for i in range(field.shape[0]):
            field[i, rows] = exact[:, i * 128 : (i + 1) * 128].astype(jnp.bfloat16)
        for i in range(field8.shape[0]):
            field8[i, rows] = cross[:, i * 128 : (i + 1) * 128].astype(F8)
    factor = factor * (1.0 / PLANAR_SCALE)

    def sample(pair, carry):
        pad = jnp.zeros((pad_rows, 128), jnp.bfloat16)
        slabs = [tables[pair * 2 + i] for i in range(2)]
        slabs = [jnp.concatenate([slab, slab[COARSE : tile.rows], pad], axis=0) for slab in slabs]
        column = jnp.dot(
            jnp.concatenate([field[i] for i in range(field.shape[0])], axis=1),
            jnp.concatenate(slabs, axis=1),
            preferred_element_type=jnp.float32,
        )
        column = column + jnp.dot(
            jnp.concatenate([field8[i] for i in range(field8.shape[0])], axis=1),
            jnp.concatenate([tables8[pair * 2 + i] for i in range(2)], axis=1),
            preferred_element_type=jnp.float32,
        )
        for i in range(2):
            vertical = verticals[pair * 2 + i]
            for k in range(3):
                part = column[k * tile.nz : (k + 1) * tile.nz, i * 128 : (i + 1) * 128]
                value = jnp.sum(part * vertical, axis=0, keepdims=True)
                slip[k, pl.ds(pair * 2 + i, 1)] = value
        return carry

    lax.fori_loop(0, total // 2, sample, 0, unroll=8)
    live = record_row(arrivals, 10, blocks)
    for k in range(3):
        slip[k, :slots] = (slip[k, :slots] * factor - velocity[k]) * stays[...]
        slip[k, slots:] = (slip[k, slots:] * factor - record_row(arrivals, 3 + k, blocks)) * live
    leave.wait()


def exchange_x(buffer, axis, count):
    forward = [(i, (i + 1) % count) for i in range(count)]
    backward = [(target, source) for source, target in forward]
    if count == 2:
        return lax.ppermute(buffer, axis, forward)
    return jnp.stack(
        [lax.ppermute(buffer[0], axis, backward), lax.ppermute(buffer[1], axis, forward)]
    )


def exchange_y(send_a, send_b, axis, count):
    if count % 2:
        perm_a = [(i, (i + 1) % count) for i in range(count)]
        perm_b = [(target, source) for source, target in perm_a]
    else:
        perm_a = [(i, i ^ 1) for i in range(count)]
        perm_b = [(i, (i + 1) % count if i % 2 else (i - 1) % count) for i in range(count)]
    return lax.ppermute(send_a, axis, perm_a), lax.ppermute(send_b, axis, perm_b)


def on_device(count_x, count_y, handoff, cells, offsets, drag, bubble_velocity, gas):
    tile = Tile(gas.shape[1], gas.shape[2], gas.shape[3])
    slots, lanes = cells.shape[2], cells.shape[3]
    codes = handoff.reshape(slots)
    cells = cells.reshape(slots, lanes)
    offsets = offsets.reshape(slots, 3, lanes).transpose(1, 0, 2)
    drag = drag.reshape(slots, 3, lanes).transpose(1, 0, 2)
    velocity = bubble_velocity.reshape(slots, 3, lanes).transpose(1, 0, 2)
    gas_rows = gas.reshape(3 * tile.wx * tile.wy, tile.nz)
    per_x, per_y = tile.wx // REC, tile.wy // REC
    bind = functools.partial
    macs = tile.rows * 3 * tile.nz * 3 * 2 * lanes

    inputs = [cells, offsets, drag, velocity, gas_rows]
    ty_shape = (3 * CAP + 3 * per_x, REC, lanes)
    send_a, send_b, own, stays, cells, offsets, drag, velocity, gas_rows = call(
        bind(pack_kernel, tile, "ty", count_y, slots),
        [ty_shape, ty_shape, (2, CAP, REC, lanes), (slots, lanes)]
        + [(value.shape, value.dtype) for value in inputs],
        [codes, *inputs],
        [HBM] * 6,
        scratch=[
            pltpu.SMEM((slots,), jnp.int32),
            pltpu.SMEM((slots + 1,), jnp.int32),
            pltpu.SMEM((9,), jnp.int32),
            pltpu.SemaphoreType.DMA((6,)),
        ],
        name="pack",
    )
    recv_a, recv_b = exchange_y(send_a, send_b, "ty", count_y)
    cut = slots * 2 // 3 // 4 * 4
    (acc,) = call(
        bind(first_kernel, tile, cut),
        [(tile.rows, 3 * tile.nz)],
        [cells, offsets, drag, stays],
        scratch=table_scratch(tile, cut),
        cost=(macs * cut, cut * lanes * 40),
        name="deposit_first",
    )
    (xsend,) = call(
        bind(join_kernel, tile, "ty", count_y),
        [(2, 3 * CAP + 3 * per_y + 1, REC, lanes)],
        [recv_a, recv_b, own, gas_rows, acc],
        [VMEM] * 4 + [ANY],
        name="join",
    )
    xrecv = exchange_x(xsend, "tx", count_x)
    (acc,) = call(
        bind(second_kernel, tile, cut, slots - cut),
        [acc.shape],
        [cells, offsets, drag, stays, acc, xsend],
        [VMEM] * 5 + [ANY],
        scratch=table_scratch(tile, slots - cut),
        cost=(macs * (slots - cut), (slots - cut) * lanes * 40),
        name="deposit_second",
    )
    edge_shape = (tile.edge_rows, tile.nz)
    blocks = 8 * CAP
    acc, arrivals, edge_a, edge_b = call(
        bind(arrive_kernel, tile, "ty", count_y),
        [acc.shape, (blocks * REC, lanes), edge_shape, edge_shape],
        [recv_a, recv_b, xrecv, acc],
        scratch=table_scratch(tile, blocks),
        cost=(macs * blocks, blocks * lanes * 40),
        name="deposit_arrivals",
    )
    got_a, got_b = exchange_y(edge_a, edge_b, "ty", count_y)
    total = slots + blocks
    fine = tile.rows - COARSE
    tables, tables8, verticals = call(
        bind(tables_kernel, tile, slots),
        [
            ((total, tile.rows + fine, lanes), jnp.bfloat16),
            ((total, 2 * COARSE, lanes), F8),
            (total, tile.nz, lanes),
        ],
        [cells, offsets, arrivals],
        scratch=[
            pltpu.VMEM((8, total, lanes), jnp.float32),
            pltpu.VMEM((total * COLS, lanes), jnp.float32),
        ],
        cost=(macs * total // 2, total * lanes * 40),
        name="tables",
    )
    mid, beyond, xedge = call(
        bind(widen_kernel, tile, "ty", count_y),
        [
            (3, tile.yw, tile.wx, tile.nz),
            (3, 2, tile.yp, tile.nz),
            (2, round_up(3 * tile.yw * EDGE, SUB), tile.nz),
        ],
        [acc, got_a, got_b, verticals],
        [VMEM] * 3 + [ANY],
        name="widen",
    )
    xgot = exchange_x(xedge, "tx", count_x)
    wide = (3, tile.yw, round_up(tile.wx + SUB + SWEEPS + SUB, SUB), tile.nz)
    gas_new, slip = call(
        bind(finish_kernel, tile, "ty", count_y, slots),
        [gas_rows.shape, (3, total, lanes)],
        [stays, velocity, gas_rows, xrecv, recv_a, recv_b, arrivals]
        + [tables, tables8, verticals, mid, beyond, xgot],
        scratch=[
            *[pltpu.VMEM(wide, jnp.float32)] * 3,
            pltpu.VMEM(((COARSE + round_up(3 * fine, 128)) // 128, 3 * tile.nz, 128), jnp.bfloat16),
            pltpu.VMEM((2 * COARSE // 128, 3 * tile.nz, 128), F8),
            pltpu.VMEM((3, tile.rows, tile.nz), jnp.float32),
            pltpu.VMEM(gas_rows.shape, jnp.float32),
            pltpu.SemaphoreType.DMA(()),
        ],
        out_specs=[HBM, VMEM],
        cost=(macs * total, total * lanes * 40),
        name="finish",
        results=True,
    )
    return gas_new.reshape(gas.shape), slip.transpose(1, 0, 2).reshape(1, 1, total, 3, lanes)


def solution(mesh):
    return jax.shard_map(
        functools.partial(on_device, mesh.shape["tx"], mesh.shape["ty"]),
        mesh=mesh,
        in_specs=(
            P("tx", "ty", None, None),
            P("tx", "ty", None, None),
            P("tx", "ty", None, None, None),
            P("tx", "ty", None, None, None),
            P("tx", "ty", None, None, None),
            P(None, "tx", "ty", None),
        ),
        out_specs=(P(None, "tx", "ty", None), P("tx", "ty", None, None, None)),
        check_vma=False,
    )
```

```python
import functools

import jax
import jax.numpy as jnp
from jax import lax
from jax.experimental import pallas as pl
from jax.experimental.pallas import tpu as pltpu
from jax.sharding import PartitionSpec as P

SWEEPS = 4
CAP = 2
DIFFUSE = 1.0
STEP_SIZE = 2.0

REC = 16
STAY = 4
REACH = SWEEPS + 1
EDGE = REACH + 1
SUB = 8
VMEM = pl.BlockSpec(memory_space=pltpu.VMEM)
SMEM = pl.BlockSpec(memory_space=pltpu.SMEM)
HBM = pl.BlockSpec(memory_space=pltpu.HBM)
ANY = pl.BlockSpec(memory_space=pl.ANY)
F8 = jnp.float8_e4m3fn
PEAK = 400.0
PLANAR_SCALE = 512.0
TINY = 1e-20
COARSE = 256
LIMIT = 24 * 1024 * 1024
COLS = 16


def round_up(count, unit):
    return -(-count // unit) * unit


def call(
    body, outs, args, specs=None, out_specs=None, scratch=(), cost=(0, 0), name=None, results=False
):
    specs = specs or [VMEM] * len(args)
    kind = jax.ShapeDtypeStruct if results else pltpu.VMEM
    return pl.pallas_call(
        body,
        out_shape=[
            kind(*out) if isinstance(out[0], tuple) else kind(out, jnp.float32) for out in outs
        ],
        in_specs=specs,
        out_specs=out_specs or [VMEM] * len(outs),
        scratch_shapes=list(scratch),
        compiler_params=pltpu.CompilerParams(vmem_limit_bytes=LIMIT),
        cost_estimate=pl.CostEstimate(flops=cost[0], bytes_accessed=cost[1], transcendentals=0),
        name=name,
    )(
        *[
            arg if spec in (SMEM, ANY) else pltpu.with_memory_space_constraint(arg, spec.memory_space)
            for arg, spec in zip(args, specs)
        ]
    )


def split_by(value, size):
    if size & (size - 1) == 0:
        return value >> (size.bit_length() - 1), value & (size - 1)
    return value // size, value % size


class Tile:
    def __init__(self, wx, wy, nz):
        self.wx, self.wy, self.nz = wx, wy, nz
        self.ye = wy + 2
        self.hp = round_up(self.ye, SUB)
        self.main = self.ye * wx
        self.rows = self.main + 2 * self.hp
        self.rows8 = round_up(self.rows, 4 * SUB)
        self.yw = wy + 2 * REACH
        self.yp = round_up(self.yw, SUB)
        self.edge_main = EDGE * wx
        self.edge_rows = round_up(3 * (self.edge_main + 2 * EDGE), SUB)

    def decode(self, cell):
        cx, rest = split_by(cell, self.wy * self.nz)
        cy, cz = split_by(rest, self.nz)
        return cx, cy, cz

    def prepare(self, first, cell, sixteenths, fields, columns, force=None):
        count = cell.shape[0]
        cx, cy, cz = self.decode(cell)
        rows = slice(first, first + count)
        fields[0, rows] = cx.astype(jnp.float32)
        fields[1, rows] = cy.astype(jnp.float32)
        for axis in range(2):
            scale = 1.0 if axis else PLANAR_SCALE
            for i, weight in enumerate(tsc_weights(sixteenths[axis])):
                fields[2 + 3 * axis + i, rows] = weight * scale
        below = jnp.where(cz == 0, self.nz - 1, cz - 1).astype(jnp.float32)
        above = jnp.where(cz == self.nz - 1, 0, cz + 1).astype(jnp.float32)
        values = [below, cz.astype(jnp.float32), above, *tsc_weights(sixteenths[2])]
        if force is not None:
            values += force
        for i, value in enumerate(values):
            columns[pl.ds(first * COLS + i, count, stride=COLS), :] = value

    def vertical(self, columns, slot):
        start = slot * COLS if isinstance(slot, int) else pl.multiple_of(slot * COLS, COLS)
        rows = [columns[pl.ds(start, COLS), :][j : j + 1] for j in range(9)]
        iz = lax.broadcasted_iota(jnp.int32, (self.nz, rows[0].shape[1]), 0).astype(jnp.float32)
        tz = jnp.where(iz == rows[2], rows[5], 0.0)
        tz = jnp.where(iz == rows[1], rows[4], tz)
        return jnp.where(iz == rows[0], rows[3], tz), rows[6:9]

    def planar(self, fields, slot):
        lanes = fields.shape[2]
        cx, cy, *weights = [fields[i, pl.ds(slot, 1), :] for i in range(8)]
        ix = lax.broadcasted_iota(jnp.int32, (self.wx, lanes), 0).astype(jnp.float32)
        tx = jnp.where(ix == cx + 1.0, weights[2], 0.0)
        tx = jnp.where(ix == cx, weights[1], tx)
        tx = jnp.where(ix == cx - 1.0, weights[0], tx)
        iy = lax.broadcasted_iota(jnp.int32, (self.hp, lanes), 0).astype(jnp.float32)
        ty = jnp.where(iy == cy + 2.0, weights[5], 0.0)
        ty = jnp.where(iy == cy + 1.0, weights[4], ty)
        ty = jnp.where(iy == cy, weights[3], ty)
        beyond_low = jnp.where(cx == 0.0, weights[0], 0.0)
        beyond_high = jnp.where(cx == self.wx - 1.0, weights[2], 0.0)
        parts = [
            jnp.concatenate([tx * ty[j : j + 1], tx * ty[j + 1 : j + 2]], axis=0)
            for j in range(0, self.ye, 2)
        ]
        return parts + [jnp.concatenate([ty * beyond_low, ty * beyond_high], axis=0)]


def tsc_weights(sixteenths):
    fraction = (sixteenths + 0.5) * (1.0 / 16.0) - 0.5
    low = 0.5 - fraction
    high = 0.5 + fraction
    return 0.5 * low * low, 0.75 - fraction * fraction, 0.5 * high * high


def halves(value):
    top = value.astype(jnp.bfloat16)
    return top, value - top.astype(jnp.float32)


def scaled(values, bound):
    peak = functools.reduce(jnp.maximum, [jnp.abs(value) for value in values])
    peak = jnp.maximum(jnp.max(peak, keepdims=True), TINY)
    factor = (PEAK / bound) / peak
    return [value * factor for value in values], peak * (bound / PEAK)


def pipeline(steps, build, use):
    build(0, 0)
    for step in range(steps):
        use(step % 2, step)
        if step + 1 < steps:
            build((step + 1) % 2, step + 1)


def deposit(tile, slots, fields, columns, acc, cross, left, left8, right, right8):
    def build(buffer, step):
        for i in range(2):
            slot = step * 2 + i
            row = 0
            for part in tile.planar(fields, slot):
                top, low = halves(part)
                rows = slice(row, row + part.shape[0])
                left[buffer][i, rows] = top
                left8[buffer][i, rows] = part.astype(F8)
                left8[buffer][2 + i, rows] = low.astype(F8)
                row += part.shape[0]
            tz, force = tile.vertical(columns, slot)
            for k in range(3):
                value = (tz * force[k]).T
                top, low = halves(value)
                right[buffer][3 * i + k] = top
                right8[buffer][3 * i + k] = low.astype(F8)
                right8[buffer][3 * (2 + i) + k] = value.astype(F8)

    def use(buffer, step):
        def pieces(a_ref, b_ref, count):
            b = [jnp.concatenate([b_ref[3 * i + k] for k in range(3)], axis=1) for i in range(count)]
            return jnp.dot(
                jnp.concatenate([a_ref[i] for i in range(count)], axis=1),
                jnp.concatenate(b, axis=0),
                preferred_element_type=jnp.float32,
            )

        exact = pieces(left[buffer], right[buffer], 2)
        coarse = pieces(left8[buffer], right8[buffer], 4)
        acc[...] = acc[...] + exact if step else exact
        cross[...] = cross[...] + coarse if step else coarse

    pipeline(slots // 2, build, use)


def ty_roles(axis, count):
    if count % 2:
        return True, False
    even = lax.axis_index(axis) % 2 == 0
    return even, even


def if_(cond, then, other):
    if isinstance(cond, bool):
        (then if cond else other)()
        return
    pl.when(cond)(then)
    pl.when(jnp.logical_not(cond))(other)


def pack_kernel(
    tile, axis, count, slots, codes_in, cells_in, offsets_in, drag_in, velocity_in, gas_in,
    send_a, send_b, own, stays, cells, offsets, drag, velocity, gas, codes, leaving, counts, sems,
):
    sources = (codes_in, cells_in, offsets_in, drag_in, velocity_in, gas_in)
    targets = (codes, cells, offsets, drag, velocity, gas)
    copies = [
        pltpu.make_async_copy(source, target, sems.at[i])
        for i, (source, target) in enumerate(zip(sources, targets))
    ]
    for copy in copies:
        copy.start()
    for ref in (send_a, send_b):
        ref[: 3 * CAP] = jnp.zeros((3 * CAP, REC, 128), jnp.float32)
    own[...] = jnp.zeros(own.shape, jnp.float32)
    for code in range(9):
        counts[code] = 0
    copies[0].wait()
    total = 0
    for slot in range(slots):
        code = codes[slot]
        stays[slot : slot + 1] = jnp.full((1, 128), (code == STAY).astype(jnp.float32), jnp.float32)
        leaving[total] = slot
        total = total + (code != STAY).astype(jnp.int32)
    for copy in copies[1:]:
        copy.wait()
    a_high, _ = ty_roles(axis, count)
    per = tile.wx // REC

    def edges(ref, high):
        y = tile.wy - 1 if high else 0
        for k in range(3):
            for part in range(per):
                start = (k * tile.wx + part * REC) * tile.wy + y
                ref[3 * CAP + k * per + part] = gas[pl.ds(start, REC, stride=tile.wy), :]

    def visit(index, carry):
        slot = leaving[index]
        code = codes[slot]
        rank = jnp.minimum(counts[code], CAP - 1)
        counts[code] = rank + 1
        here = pl.ds(slot, 1)

        def put(ref):
            for k in range(3):
                ref[k : k + 1] = drag[k, here]
                ref[3 + k : 4 + k] = velocity[k, here]
                ref[7 + k : 8 + k] = offsets[k, here].astype(jnp.float32)
            ref[6:7] = cells[here].astype(jnp.float32)
            ref[10:11] = jnp.ones((1, 128), jnp.float32)

        row = (code >= 3).astype(jnp.int32) + (code >= 6).astype(jnp.int32)
        column = code - 3 * row
        to_a = (column == 2) == a_high
        place = row * CAP + rank
        pl.when(column == 1)(lambda: put(own.at[(row >= 1).astype(jnp.int32), rank]))
        pl.when((column != 1) & to_a)(lambda: put(send_a.at[place]))
        pl.when((column != 1) & jnp.logical_not(to_a))(lambda: put(send_b.at[place]))
        return carry

    lax.fori_loop(0, total, visit, 0)
    if_(
        a_high,
        lambda: (edges(send_a, True), edges(send_b, False)) and None,
        lambda: (edges(send_a, False), edges(send_b, True)) and None,
    )


def join_kernel(tile, axis, count, recv_a, recv_b, own, gas, acc, xsend):
    _, a_from_high = ty_roles(axis, count)
    per_x, per_y = tile.wx // REC, tile.wy // REC
    corner = 3 * CAP + 3 * per_y
    for side, x in ((0, 0), (1, tile.wx - 1)):
        xsend[side, corner] = jnp.zeros((REC, 128), jnp.float32)
        for s in range(CAP):
            xsend[side, CAP + s] = own[side, s]
        for k in range(3):
            for part in range(per_y):
                start = (k * tile.wx + x) * tile.wy + part * REC
                xsend[side, 3 * CAP + k * per_y + part] = gas[start : start + REC]

    def forward(ref, high):
        first = 2 * CAP if high else 0
        for side, x in ((0, 0), (1, tile.wx - 1)):
            for s in range(CAP):
                xsend[side, first + s] = ref[2 * CAP * side + s]
            for k in range(3):
                place = 3 * CAP + k * per_x + x // REC
                row = 2 * k + int(high)
                xsend[side, corner, row : row + 1] = ref[place, x % REC : x % REC + 1]

    if_(
        a_from_high,
        lambda: (forward(recv_a, True), forward(recv_b, False)) and None,
        lambda: (forward(recv_a, False), forward(recv_b, True)) and None,
    )


def table_scratch(tile, slots):
    rows, turned = (tile.rows, 128), (128, tile.nz)
    return [
        pltpu.VMEM((8, slots, 128), jnp.float32),
        pltpu.VMEM((slots * COLS, 128), jnp.float32),
        *[pltpu.VMEM((2, *rows), jnp.bfloat16)] * 2,
        *[pltpu.VMEM((4, tile.rows8, 128), F8)] * 2,
        *[pltpu.VMEM((6, *turned), jnp.bfloat16)] * 2,
        *[pltpu.VMEM((12, *turned), F8)] * 2,
        pltpu.VMEM((tile.rows8, 3 * tile.nz), jnp.float32),
    ]


def deposit_blocks(tile, cell, sixteenths, force, acc, fields, columns, *buffers):
    force, factor = scaled(force, 0.75)
    tile.prepare(0, cell, sixteenths, fields, columns, force)
    cross = buffers[8]
    pairs = [buffers[i : i + 2] for i in range(0, 8, 2)]
    for buffer in pairs[1]:
        buffer[:, tile.rows :] = jnp.zeros((4, tile.rows8 - tile.rows, 128), F8)
    deposit(tile, cell.shape[0], fields, columns, acc, cross, *pairs)
    acc[...] += cross[: tile.rows]
    return factor * (1.0 / PLANAR_SCALE)


def own_blocks(tile, first, count, cells, offsets, drag, stays, acc, *scratch):
    rows = slice(first, first + count)
    sixteenths = [offsets[k, rows].astype(jnp.float32) for k in range(3)]
    force = [drag[k, rows] * stays[rows] for k in range(3)]
    return deposit_blocks(tile, cells[rows], sixteenths, force, acc, *scratch)


def first_kernel(tile, count, cells, offsets, drag, stays, acc, *scratch):
    factor = own_blocks(tile, 0, count, cells, offsets, drag, stays, acc, *scratch)
    acc[...] = acc[...] * factor


def second_kernel(tile, first, count, cells, offsets, drag, stays, acc_in, xsend, acc, *scratch):
    factor = own_blocks(tile, first, count, cells, offsets, drag, stays, acc, *scratch)
    acc[...] = acc_in[...] + acc[...] * factor


def record_row(records, row, count):
    return records[pl.ds(row, count, stride=REC), :]


def arrive_kernel(
    tile, axis, count, recv_a, recv_b, xrecv, acc_in, acc, arrivals, send_a, send_b, *scratch
):
    a_high, a_from_high = ty_roles(axis, count)

    def place(j, record):
        arrivals[j * REC : (j + 1) * REC] = record

    for i in range(3 * CAP):
        place(i, xrecv[1, i])
        place(5 * CAP + i, xrecv[0, i])

    def middle(ref, j):
        for s in range(CAP):
            place(j * CAP + s, ref[CAP + s])

    if_(
        a_from_high,
        lambda: (middle(recv_a, 4), middle(recv_b, 3)) and None,
        lambda: (middle(recv_a, 3), middle(recv_b, 4)) and None,
    )
    blocks = 8 * CAP
    live = record_row(arrivals, 10, blocks)
    force = [record_row(arrivals, k, blocks) * live for k in range(3)]
    sixteenths = [record_row(arrivals, 7 + k, blocks) for k in range(3)]
    cell = record_row(arrivals, 6, blocks).astype(jnp.int32)
    factor = deposit_blocks(tile, cell, sixteenths, force, acc, *scratch)
    acc[...] = acc_in[...] + acc[...] * factor

    def edge(ref, high):
        first = tile.ye - EDGE if high else 0
        tail = 3 * tile.edge_main
        for k in range(3):
            lanes = slice(k * tile.nz, (k + 1) * tile.nz)
            ref[k * tile.edge_main : (k + 1) * tile.edge_main] = acc[
                first * tile.wx : (first + EDGE) * tile.wx, lanes
            ]
            for h in range(2):
                start = tile.main + h * tile.hp + first
                row = tail + (2 * k + h) * EDGE
                ref[row : row + EDGE] = acc[start : start + EDGE, lanes]

    def even():
        edge(send_a, True)
        edge(send_b, False)

    def odd():
        edge(send_a, False)
        edge(send_b, True)

    for ref in (send_a, send_b):
        last = tile.edge_rows - SUB
        ref[last:] = jnp.zeros((SUB, tile.nz), jnp.float32)
    if_(a_high, even, odd)


def widen_kernel(tile, axis, count, acc, recv_a, recv_b, verticals, mid, beyond, xsend):
    _, a_from_high = ty_roles(axis, count)
    own = slice(REACH - 1, REACH - 1 + tile.ye)
    for k in range(3):
        lanes = slice(k * tile.nz, (k + 1) * tile.nz)
        zero = jnp.zeros((REACH - 1, tile.wx, tile.nz), jnp.float32)
        mid[k, : REACH - 1] = zero
        mid[k, REACH - 1 + tile.ye :] = zero
        mid[k, own] = acc[: tile.main, lanes].reshape(tile.ye, tile.wx, tile.nz)
        for h in range(2):
            start = tile.main + h * tile.hp
            beyond[k, h] = jnp.zeros((tile.yp, tile.nz), jnp.float32)
            beyond[k, h, own] = acc[start : start + tile.ye, lanes]

    def add(ref, high):
        first = tile.yw - EDGE if high else 0
        tail = 3 * tile.edge_main
        for k in range(3):
            rows = ref[k * tile.edge_main : (k + 1) * tile.edge_main]
            mid[k, first : first + EDGE] += rows.reshape(EDGE, tile.wx, tile.nz)
            for h in range(2):
                row = tail + (2 * k + h) * EDGE
                beyond[k, h, first : first + EDGE] += ref[row : row + EDGE]

    if_(
        a_from_high,
        lambda: (add(recv_a, True), add(recv_b, False)) and None,
        lambda: (add(recv_a, False), add(recv_b, True)) and None,
    )
    for k in range(3):
        for y in range(tile.yw):
            row = (k * tile.yw + y) * EDGE
            xsend[0, row : row + 1] = beyond[k, 0, y : y + 1]
            xsend[0, row + 1 : row + EDGE] = mid[k, y, :REACH]
            xsend[1, row : row + REACH] = mid[k, y, tile.wx - REACH :]
            xsend[1, row + REACH : row + EDGE] = beyond[k, 1, y : y + 1]


def stack_gas(tile, a_from_high, gas, xgas, ygas_a, ygas_b, stack):
    per_x, per_y = tile.wx // REC, tile.wy // REC

    def take_edges(ref, high):
        y = tile.ye - 1 if high else 0
        for k in range(3):
            for part in range(per_x):
                row = y * tile.wx + part * REC
                stack[k, row : row + REC] = ref[3 * CAP + k * per_x + part]
    for k in range(3):
        for h in range(2):
            start = tile.main + h * tile.hp
            stack[k, start : start + tile.hp] = jnp.zeros((tile.hp, tile.nz), jnp.float32)
            for part in range(per_y):
                row = start + 1 + part * REC
                stack[k, row : row + REC] = xgas[1 - h, 3 * CAP + k * per_y + part]
            corner = 3 * CAP + 3 * per_y
            stack[k, start : start + 1] = xgas[1 - h, corner, 2 * k : 2 * k + 1]
            last = start + tile.ye - 1
            stack[k, last : last + 1] = xgas[1 - h, corner, 2 * k + 1 : 2 * k + 2]
        for y in range(tile.wy):
            stack[k, (y + 1) * tile.wx : (y + 2) * tile.wx] = gas[
                pl.ds(k * tile.wx * tile.wy + y, tile.wx, stride=tile.wy), :
            ]
    if_(
        a_from_high,
        lambda: (take_edges(ygas_a, True), take_edges(ygas_b, False)) and None,
        lambda: (take_edges(ygas_a, False), take_edges(ygas_b, True)) and None,
    )


def tables_kernel(
    tile, axis, count, slots, cells, offsets, arrivals, gas, xgas, ygas_a, ygas_b,
    tables, tables8, verticals, stack, fields, columns,
):
    blocks = 8 * CAP
    tile.prepare(0, cells[...], [offsets[k].astype(jnp.float32) for k in range(3)], fields, columns)
    sixteenths = [record_row(arrivals, 7 + k, blocks) for k in range(3)]
    cell = record_row(arrivals, 6, blocks).astype(jnp.int32)
    tile.prepare(slots, cell, sixteenths, fields, columns)

    def build(pair, carry):
        for i in range(2):
            slot = pair * 2 + i
            row = 0
            for part in tile.planar(fields, slot):
                top, low = halves(part)
                height = part.shape[0]
                tables[slot, row : row + height] = top
                if row < COARSE:
                    tables8[slot, row : row + height] = part.astype(F8)
                    tables8[slot, COARSE + row : COARSE + row + height] = low.astype(F8)
                else:
                    down = tile.rows - COARSE + row
                    tables[slot, down : down + height] = low.astype(jnp.bfloat16)
                row += height
            verticals[slot], _ = tile.vertical(columns, slot)
        return carry

    lax.fori_loop(0, (slots + blocks) // 2, build, 0)
    _, a_from_high = ty_roles(axis, count)
    stack_gas(tile, a_from_high, gas, xgas, ygas_a, ygas_b, stack)


def finish_kernel(
    tile, slots, stays, velocity, arrivals, tables, tables8, verticals, stack,
    mid, beyond, xrecv, gas_out, slip, src, ping, pong, field, field8, ext, gas_new, sem,
):
    zero = SUB + SWEEPS
    after = zero + tile.wx
    swept = tile.wx + 2 * SWEEPS
    for k in range(3):
        for y in range(tile.yw):
            row = (k * tile.yw + y) * EDGE
            src[k, y, zero - SUB : zero] = jnp.zeros((SUB, tile.nz), jnp.float32)
            src[k, y, zero:after] = mid[k, y]
            src[k, y, after : after + SUB] = jnp.zeros((SUB, tile.nz), jnp.float32)
            src[k, y, zero - REACH : zero] = xrecv[1, row : row + REACH]
            src[k, y, after : after + REACH] = xrecv[0, row + 1 : row + EDGE]
            src[k, y, zero - 1 : zero] += beyond[k, 0, y : y + 1]
            src[k, y, after : after + 1] += beyond[k, 1, y : y + 1]
            src[k, y, zero : zero + 1] += xrecv[1, row + REACH : row + EDGE]
            src[k, y, after - 1 : after] += xrecv[0, row : row + 1]

    def sweep(old, new, margin):
        def row(y):
            for k in range(3):
                here = old[k, y, SUB : SUB + swept]
                around = old[k, y - 1, SUB : SUB + swept] + old[k, y + 1, SUB : SUB + swept]
                around = around + old[k, y, SUB - 1 : SUB - 1 + swept]
                around = around + old[k, y, SUB + 1 : SUB + 1 + swept]
                around = around + pltpu.roll(here, 1, 1) + pltpu.roll(here, tile.nz - 1, 1)
                total = src[k, y, SUB : SUB + swept] + DIFFUSE * around
                new[k, y, SUB : SUB + swept] = total * (1.0 / (1.0 + 6.0 * DIFFUSE))

        for y in range(margin, tile.yw - margin):
            row(y)

    buffers = [src, ping, pong, ping, pong]
    for index in range(SWEEPS):
        sweep(buffers[index], buffers[index + 1], index + 1)
    filtered = buffers[SWEEPS]

    for k in range(3):
        ext[k, tile.main :] = stack[k, tile.main :]
        for y in range(tile.ye):
            rows = slice(y * tile.wx, (y + 1) * tile.wx)
            updated = stack[k, rows] + STEP_SIZE * filtered[k, y + REACH - 1, zero:after]
            ext[k, rows] = updated
            if 1 <= y <= tile.wy:
                gas_new[pl.ds(k * tile.wx * tile.wy + y - 1, tile.wx, stride=tile.wy), :] = updated
            for h, x in ((0, zero - 1), (1, after)):
                row = tile.main + h * tile.hp + y
                ext[k, row : row + 1] += STEP_SIZE * filtered[k, y + REACH - 1, x : x + 1]
    leave = pltpu.make_async_copy(gas_new, gas_out, sem)
    leave.start()
    blocks = 8 * CAP
    total = slots + blocks
    fine = tile.rows - COARSE
    pad_rows = round_up(3 * fine, 128) - 3 * fine
    values, factor = scaled([ext[k] for k in range(3)], 1.0)
    for k, value in enumerate(values):
        top = value.astype(jnp.bfloat16).astype(jnp.float32)
        low = value - top
        pad = jnp.zeros((pad_rows, tile.nz), jnp.float32)
        exact = jnp.concatenate([top, top[COARSE:], low[COARSE:], pad], axis=0).T
        cross = jnp.concatenate([low[:COARSE], value[:COARSE]], axis=0).T
        rows = slice(k * tile.nz, (k + 1) * tile.nz)
        for i in range(field.shape[0]):
            field[i, rows] = exact[:, i * 128 : (i + 1) * 128].astype(jnp.bfloat16)
        for i in range(field8.shape[0]):
            field8[i, rows] = cross[:, i * 128 : (i + 1) * 128].astype(F8)
    factor = factor * (1.0 / PLANAR_SCALE)

    def sample(pair, carry):
        pad = jnp.zeros((pad_rows, 128), jnp.bfloat16)
        slabs = [tables[pair * 2 + i] for i in range(2)]
        slabs = [jnp.concatenate([slab, slab[COARSE : tile.rows], pad], axis=0) for slab in slabs]
        column = jnp.dot(
            jnp.concatenate([field[i] for i in range(field.shape[0])], axis=1),
            jnp.concatenate(slabs, axis=1),
            preferred_element_type=jnp.float32,
        )
        column = column + jnp.dot(
            jnp.concatenate([field8[i] for i in range(field8.shape[0])], axis=1),
            jnp.concatenate([tables8[pair * 2 + i] for i in range(2)], axis=1),
            preferred_element_type=jnp.float32,
        )
        for i in range(2):
            vertical = verticals[pair * 2 + i]
            for k in range(3):
                part = column[k * tile.nz : (k + 1) * tile.nz, i * 128 : (i + 1) * 128]
                value = jnp.sum(part * vertical, axis=0, keepdims=True)
                slip[k, pl.ds(pair * 2 + i, 1)] = value
        return carry

    lax.fori_loop(0, total // 2, sample, 0, unroll=16)
    live = record_row(arrivals, 10, blocks)
    for k in range(3):
        slip[k, :slots] = (slip[k, :slots] * factor - velocity[k]) * stays[...]
        slip[k, slots:] = (slip[k, slots:] * factor - record_row(arrivals, 3 + k, blocks)) * live
    leave.wait()


def exchange_x(buffer, axis, count):
    forward = [(i, (i + 1) % count) for i in range(count)]
    backward = [(target, source) for source, target in forward]
    if count == 2:
        return lax.ppermute(buffer, axis, forward)
    return jnp.stack(
        [lax.ppermute(buffer[0], axis, backward), lax.ppermute(buffer[1], axis, forward)]
    )


def exchange_y(send_a, send_b, axis, count):
    if count % 2:
        perm_a = [(i, (i + 1) % count) for i in range(count)]
        perm_b = [(target, source) for source, target in perm_a]
    else:
        perm_a = [(i, i ^ 1) for i in range(count)]
        perm_b = [(i, (i + 1) % count if i % 2 else (i - 1) % count) for i in range(count)]
    return lax.ppermute(send_a, axis, perm_a), lax.ppermute(send_b, axis, perm_b)


def on_device(count_x, count_y, handoff, cells, offsets, drag, bubble_velocity, gas):
    tile = Tile(gas.shape[1], gas.shape[2], gas.shape[3])
    slots, lanes = cells.shape[2], cells.shape[3]
    codes = handoff.reshape(slots)
    cells = cells.reshape(slots, lanes)
    offsets = offsets.reshape(slots, 3, lanes).transpose(1, 0, 2)
    drag = drag.reshape(slots, 3, lanes).transpose(1, 0, 2)
    velocity = bubble_velocity.reshape(slots, 3, lanes).transpose(1, 0, 2)
    gas_rows = gas.reshape(3 * tile.wx * tile.wy, tile.nz)
    per_x, per_y = tile.wx // REC, tile.wy // REC
    bind = functools.partial
    macs = tile.rows * 3 * tile.nz * 3 * 2 * lanes

    inputs = [cells, offsets, drag, velocity, gas_rows]
    ty_shape = (3 * CAP + 3 * per_x, REC, lanes)
    send_a, send_b, own, stays, cells, offsets, drag, velocity, gas_rows = call(
        bind(pack_kernel, tile, "ty", count_y, slots),
        [ty_shape, ty_shape, (2, CAP, REC, lanes), (slots, lanes)]
        + [(value.shape, value.dtype) for value in inputs],
        [codes, *inputs],
        [HBM] * 6,
        scratch=[
            pltpu.SMEM((slots,), jnp.int32),
            pltpu.SMEM((slots + 1,), jnp.int32),
            pltpu.SMEM((9,), jnp.int32),
            pltpu.SemaphoreType.DMA((6,)),
        ],
        name="pack",
    )
    recv_a, recv_b = exchange_y(send_a, send_b, "ty", count_y)
    cut = slots * 2 // 3 // 4 * 4
    (acc,) = call(
        bind(first_kernel, tile, cut),
        [(tile.rows, 3 * tile.nz)],
        [cells, offsets, drag, stays],
        scratch=table_scratch(tile, cut),
        cost=(macs * cut, cut * lanes * 40),
        name="deposit_first",
    )
    (xsend,) = call(
        bind(join_kernel, tile, "ty", count_y),
        [(2, 3 * CAP + 3 * per_y + 1, REC, lanes)],
        [recv_a, recv_b, own, gas_rows, acc],
        [VMEM] * 4 + [ANY],
        name="join",
    )
    xrecv = exchange_x(xsend, "tx", count_x)
    (acc,) = call(
        bind(second_kernel, tile, cut, slots - cut),
        [acc.shape],
        [cells, offsets, drag, stays, acc, xsend],
        [VMEM] * 5 + [ANY],
        scratch=table_scratch(tile, slots - cut),
        cost=(macs * (slots - cut), (slots - cut) * lanes * 40),
        name="deposit_second",
    )
    edge_shape = (tile.edge_rows, tile.nz)
    blocks = 8 * CAP
    acc, arrivals, edge_a, edge_b = call(
        bind(arrive_kernel, tile, "ty", count_y),
        [acc.shape, (blocks * REC, lanes), edge_shape, edge_shape],
        [recv_a, recv_b, xrecv, acc],
        scratch=table_scratch(tile, blocks),
        cost=(macs * blocks, blocks * lanes * 40),
        name="deposit_arrivals",
    )
    got_a, got_b = exchange_y(edge_a, edge_b, "ty", count_y)
    total = slots + blocks
    fine = tile.rows - COARSE
    tables, tables8, verticals, stack = call(
        bind(tables_kernel, tile, "ty", count_y, slots),
        [
            ((total, tile.rows + fine, lanes), jnp.bfloat16),
            ((total, 2 * COARSE, lanes), F8),
            (total, tile.nz, lanes),
            (3, tile.rows, tile.nz),
        ],
        [cells, offsets, arrivals, gas_rows, xrecv, recv_a, recv_b],
        scratch=[
            pltpu.VMEM((8, total, lanes), jnp.float32),
            pltpu.VMEM((total * COLS, lanes), jnp.float32),
        ],
        cost=(macs * total // 2, total * lanes * 40),
        name="tables",
    )
    mid, beyond, xedge = call(
        bind(widen_kernel, tile, "ty", count_y),
        [
            (3, tile.yw, tile.wx, tile.nz),
            (3, 2, tile.yp, tile.nz),
            (2, round_up(3 * tile.yw * EDGE, SUB), tile.nz),
        ],
        [acc, got_a, got_b, verticals],
        [VMEM] * 3 + [ANY],
        name="widen",
    )
    xgot = exchange_x(xedge, "tx", count_x)
    wide = (3, tile.yw, round_up(tile.wx + SUB + SWEEPS + SUB, SUB), tile.nz)
    gas_new, slip = call(
        bind(finish_kernel, tile, slots),
        [gas_rows.shape, (3, total, lanes)],
        [stays, velocity, arrivals, tables, tables8, verticals, stack, mid, beyond, xgot],
        scratch=[
            *[pltpu.VMEM(wide, jnp.float32)] * 3,
            pltpu.VMEM(((COARSE + round_up(3 * fine, 128)) // 128, 3 * tile.nz, 128), jnp.bfloat16),
            pltpu.VMEM((2 * COARSE // 128, 3 * tile.nz, 128), F8),
            pltpu.VMEM((3, tile.rows, tile.nz), jnp.float32),
            pltpu.VMEM(gas_rows.shape, jnp.float32),
            pltpu.SemaphoreType.DMA(()),
        ],
        out_specs=[HBM, VMEM],
        cost=(macs * total, total * lanes * 40),
        name="finish",
        results=True,
    )
    return gas_new.reshape(gas.shape), slip.transpose(1, 0, 2).reshape(1, 1, total, 3, lanes)


def solution(mesh):
    return jax.shard_map(
        functools.partial(on_device, mesh.shape["tx"], mesh.shape["ty"]),
        mesh=mesh,
        in_specs=(
            P("tx", "ty", None, None),
            P("tx", "ty", None, None),
            P("tx", "ty", None, None, None),
            P("tx", "ty", None, None, None),
            P("tx", "ty", None, None, None),
            P(None, "tx", "ty", None),
        ),
        out_specs=(P(None, "tx", "ty", None), P("tx", "ty", None, None, None)),
        check_vma=False,
    )
```

```python
import functools

import jax
import jax.numpy as jnp
from jax import lax
from jax.experimental import pallas as pl
from jax.experimental.pallas import tpu as pltpu
from jax.sharding import PartitionSpec as P

SWEEPS = 4
CAP = 2
DIFFUSE = 1.0
STEP_SIZE = 2.0

REC = 16
STAY = 4
REACH = SWEEPS + 1
EDGE = REACH + 1
SUB = 8
VMEM = pl.BlockSpec(memory_space=pltpu.VMEM)
SMEM = pl.BlockSpec(memory_space=pltpu.SMEM)
HBM = pl.BlockSpec(memory_space=pltpu.HBM)
ANY = pl.BlockSpec(memory_space=pl.ANY)
F8 = jnp.float8_e4m3fn
PEAK = 400.0
PLANAR_SCALE = 512.0
TINY = 1e-20
COARSE = 256
LIMIT = 24 * 1024 * 1024
COLS = 16


def round_up(count, unit):
    return -(-count // unit) * unit


def call(
    body, outs, args, specs=None, out_specs=None, scratch=(), cost=(0, 0), name=None, results=False
):
    specs = specs or [VMEM] * len(args)
    kind = jax.ShapeDtypeStruct if results else pltpu.VMEM
    return pl.pallas_call(
        body,
        out_shape=[
            kind(*out) if isinstance(out[0], tuple) else kind(out, jnp.float32) for out in outs
        ],
        in_specs=specs,
        out_specs=out_specs or [VMEM] * len(outs),
        scratch_shapes=list(scratch),
        compiler_params=pltpu.CompilerParams(vmem_limit_bytes=LIMIT),
        cost_estimate=pl.CostEstimate(flops=cost[0], bytes_accessed=cost[1], transcendentals=0),
        name=name,
    )(
        *[
            arg if spec in (SMEM, ANY) else pltpu.with_memory_space_constraint(arg, spec.memory_space)
            for arg, spec in zip(args, specs)
        ]
    )


def split_by(value, size):
    if size & (size - 1) == 0:
        return value >> (size.bit_length() - 1), value & (size - 1)
    return value // size, value % size


class Tile:
    def __init__(self, wx, wy, nz):
        self.wx, self.wy, self.nz = wx, wy, nz
        self.ye = wy + 2
        self.hp = round_up(self.ye, SUB)
        self.main = self.ye * wx
        self.rows = self.main + 2 * self.hp
        self.rows8 = round_up(self.rows, 4 * SUB)
        self.yw = wy + 2 * REACH
        self.yp = round_up(self.yw, SUB)
        self.edge_main = EDGE * wx
        self.edge_rows = round_up(3 * (self.edge_main + 2 * EDGE), SUB)

    def decode(self, cell):
        cx, rest = split_by(cell, self.wy * self.nz)
        cy, cz = split_by(rest, self.nz)
        return cx, cy, cz

    def prepare(self, first, cell, sixteenths, fields, columns, force=None):
        count = cell.shape[0]
        cx, cy, cz = self.decode(cell)
        rows = slice(first, first + count)
        fields[0, rows] = cx.astype(jnp.float32)
        fields[1, rows] = cy.astype(jnp.float32)
        for axis in range(2):
            scale = 1.0 if axis else PLANAR_SCALE
            for i, weight in enumerate(tsc_weights(sixteenths[axis])):
                fields[2 + 3 * axis + i, rows] = weight * scale
        below = jnp.where(cz == 0, self.nz - 1, cz - 1).astype(jnp.float32)
        above = jnp.where(cz == self.nz - 1, 0, cz + 1).astype(jnp.float32)
        values = [below, cz.astype(jnp.float32), above, *tsc_weights(sixteenths[2])]
        if force is not None:
            values += force
        for i, value in enumerate(values):
            columns[pl.ds(first * COLS + i, count, stride=COLS), :] = value

    def vertical(self, columns, slot):
        start = slot * COLS if isinstance(slot, int) else pl.multiple_of(slot * COLS, COLS)
        rows = [columns[pl.ds(start, COLS), :][j : j + 1] for j in range(9)]
        iz = lax.broadcasted_iota(jnp.int32, (self.nz, rows[0].shape[1]), 0).astype(jnp.float32)
        tz = jnp.where(iz == rows[2], rows[5], 0.0)
        tz = jnp.where(iz == rows[1], rows[4], tz)
        return jnp.where(iz == rows[0], rows[3], tz), rows[6:9]

    def planar(self, fields, slot):
        lanes = fields.shape[2]
        cx, cy, *weights = [fields[i, pl.ds(slot, 1), :] for i in range(8)]
        ix = lax.broadcasted_iota(jnp.int32, (self.wx, lanes), 0).astype(jnp.float32)
        tx = jnp.where(ix == cx + 1.0, weights[2], 0.0)
        tx = jnp.where(ix == cx, weights[1], tx)
        tx = jnp.where(ix == cx - 1.0, weights[0], tx)
        iy = lax.broadcasted_iota(jnp.int32, (self.hp, lanes), 0).astype(jnp.float32)
        ty = jnp.where(iy == cy + 2.0, weights[5], 0.0)
        ty = jnp.where(iy == cy + 1.0, weights[4], ty)
        ty = jnp.where(iy == cy, weights[3], ty)
        beyond_low = jnp.where(cx == 0.0, weights[0], 0.0)
        beyond_high = jnp.where(cx == self.wx - 1.0, weights[2], 0.0)
        parts = [
            jnp.concatenate([tx * ty[j : j + 1], tx * ty[j + 1 : j + 2]], axis=0)
            for j in range(0, self.ye, 2)
        ]
        return parts + [jnp.concatenate([ty * beyond_low, ty * beyond_high], axis=0)]


def tsc_weights(sixteenths):
    fraction = (sixteenths + 0.5) * (1.0 / 16.0) - 0.5
    low = 0.5 - fraction
    high = 0.5 + fraction
    return 0.5 * low * low, 0.75 - fraction * fraction, 0.5 * high * high


def halves(value):
    top = value.astype(jnp.bfloat16)
    return top, value - top.astype(jnp.float32)


def scaled(values, bound):
    peak = functools.reduce(jnp.maximum, [jnp.abs(value) for value in values])
    peak = jnp.maximum(jnp.max(peak, keepdims=True), TINY)
    factor = (PEAK / bound) / peak
    return [value * factor for value in values], peak * (bound / PEAK)


def pipeline(steps, build, use):
    build(0, 0)
    for step in range(steps):
        use(step % 2, step)
        if step + 1 < steps:
            build((step + 1) % 2, step + 1)


def deposit(tile, slots, fields, columns, acc, cross, left, left8, right, right8):
    def build(buffer, step):
        for i in range(2):
            slot = step * 2 + i
            row = 0
            for part in tile.planar(fields, slot):
                top, low = halves(part)
                rows = slice(row, row + part.shape[0])
                left[buffer][i, rows] = top
                left8[buffer][i, rows] = part.astype(F8)
                left8[buffer][2 + i, rows] = low.astype(F8)
                row += part.shape[0]
            tz, force = tile.vertical(columns, slot)
            for k in range(3):
                value = (tz * force[k]).T
                top, low = halves(value)
                right[buffer][3 * i + k] = top
                right8[buffer][3 * i + k] = low.astype(F8)
                right8[buffer][3 * (2 + i) + k] = value.astype(F8)

    def use(buffer, step):
        def pieces(a_ref, b_ref, count):
            b = [jnp.concatenate([b_ref[3 * i + k] for k in range(3)], axis=1) for i in range(count)]
            return jnp.dot(
                jnp.concatenate([a_ref[i] for i in range(count)], axis=1),
                jnp.concatenate(b, axis=0),
                preferred_element_type=jnp.float32,
            )

        exact = pieces(left[buffer], right[buffer], 2)
        coarse = pieces(left8[buffer], right8[buffer], 4)
        acc[...] = acc[...] + exact if step else exact
        cross[...] = cross[...] + coarse if step else coarse

    pipeline(slots // 2, build, use)


def ty_roles(axis, count):
    if count % 2:
        return True, False
    even = lax.axis_index(axis) % 2 == 0
    return even, even


def if_(cond, then, other):
    if isinstance(cond, bool):
        (then if cond else other)()
        return
    pl.when(cond)(then)
    pl.when(jnp.logical_not(cond))(other)


def pack_kernel(
    tile, axis, count, slots, codes_in, cells_in, offsets_in, drag_in, velocity_in, gas_in,
    send_a, send_b, own, stays, cells, offsets, drag, velocity, gas, codes, leaving, counts, sems,
):
    sources = (codes_in, cells_in, offsets_in, drag_in, velocity_in, gas_in)
    targets = (codes, cells, offsets, drag, velocity, gas)
    copies = [
        pltpu.make_async_copy(source, target, sems.at[i])
        for i, (source, target) in enumerate(zip(sources, targets))
    ]
    for copy in copies:
        copy.start()
    for ref in (send_a, send_b):
        ref[: 3 * CAP] = jnp.zeros((3 * CAP, REC, 128), jnp.float32)
    own[...] = jnp.zeros(own.shape, jnp.float32)
    for code in range(9):
        counts[code] = 0
    copies[0].wait()
    total = 0
    for slot in range(slots):
        code = codes[slot]
        stays[slot : slot + 1] = jnp.full((1, 128), (code == STAY).astype(jnp.float32), jnp.float32)
        leaving[total] = slot
        total = total + (code != STAY).astype(jnp.int32)
    for copy in copies[1:]:
        copy.wait()
    a_high, _ = ty_roles(axis, count)
    per = tile.wx // REC

    def edges(ref, high):
        y = tile.wy - 1 if high else 0
        for k in range(3):
            for part in range(per):
                start = (k * tile.wx + part * REC) * tile.wy + y
                ref[3 * CAP + k * per + part] = gas[pl.ds(start, REC, stride=tile.wy), :]

    def visit(index, carry):
        slot = leaving[index]
        code = codes[slot]
        rank = jnp.minimum(counts[code], CAP - 1)
        counts[code] = rank + 1
        here = pl.ds(slot, 1)

        def put(ref):
            for k in range(3):
                ref[k : k + 1] = drag[k, here]
                ref[3 + k : 4 + k] = velocity[k, here]
                ref[7 + k : 8 + k] = offsets[k, here].astype(jnp.float32)
            ref[6:7] = cells[here].astype(jnp.float32)
            ref[10:11] = jnp.ones((1, 128), jnp.float32)

        row = (code >= 3).astype(jnp.int32) + (code >= 6).astype(jnp.int32)
        column = code - 3 * row
        to_a = (column == 2) == a_high
        place = row * CAP + rank
        pl.when(column == 1)(lambda: put(own.at[(row >= 1).astype(jnp.int32), rank]))
        pl.when((column != 1) & to_a)(lambda: put(send_a.at[place]))
        pl.when((column != 1) & jnp.logical_not(to_a))(lambda: put(send_b.at[place]))
        return carry

    lax.fori_loop(0, total, visit, 0)
    if_(
        a_high,
        lambda: (edges(send_a, True), edges(send_b, False)) and None,
        lambda: (edges(send_a, False), edges(send_b, True)) and None,
    )


def join_kernel(tile, axis, count, recv_a, recv_b, own, gas, acc, xsend):
    _, a_from_high = ty_roles(axis, count)
    per_x, per_y = tile.wx // REC, tile.wy // REC
    corner = 3 * CAP + 3 * per_y
    for side, x in ((0, 0), (1, tile.wx - 1)):
        xsend[side, corner] = jnp.zeros((REC, 128), jnp.float32)
        for s in range(CAP):
            xsend[side, CAP + s] = own[side, s]
        for k in range(3):
            for part in range(per_y):
                start = (k * tile.wx + x) * tile.wy + part * REC
                xsend[side, 3 * CAP + k * per_y + part] = gas[start : start + REC]

    def forward(ref, high):
        first = 2 * CAP if high else 0
        for side, x in ((0, 0), (1, tile.wx - 1)):
            for s in range(CAP):
                xsend[side, first + s] = ref[2 * CAP * side + s]
            for k in range(3):
                place = 3 * CAP + k * per_x + x // REC
                row = 2 * k + int(high)
                xsend[side, corner, row : row + 1] = ref[place, x % REC : x % REC + 1]

    if_(
        a_from_high,
        lambda: (forward(recv_a, True), forward(recv_b, False)) and None,
        lambda: (forward(recv_a, False), forward(recv_b, True)) and None,
    )


def table_scratch(tile, slots):
    rows, turned = (tile.rows, 128), (128, tile.nz)
    return [
        pltpu.VMEM((8, slots, 128), jnp.float32),
        pltpu.VMEM((slots * COLS, 128), jnp.float32),
        *[pltpu.VMEM((2, *rows), jnp.bfloat16)] * 2,
        *[pltpu.VMEM((4, tile.rows8, 128), F8)] * 2,
        *[pltpu.VMEM((6, *turned), jnp.bfloat16)] * 2,
        *[pltpu.VMEM((12, *turned), F8)] * 2,
        pltpu.VMEM((tile.rows8, 3 * tile.nz), jnp.float32),
    ]


def deposit_blocks(tile, cell, sixteenths, force, acc, fields, columns, *buffers):
    force, factor = scaled(force, 0.75)
    tile.prepare(0, cell, sixteenths, fields, columns, force)
    cross = buffers[8]
    pairs = [buffers[i : i + 2] for i in range(0, 8, 2)]
    for buffer in pairs[1]:
        buffer[:, tile.rows :] = jnp.zeros((4, tile.rows8 - tile.rows, 128), F8)
    deposit(tile, cell.shape[0], fields, columns, acc, cross, *pairs)
    acc[...] += cross[: tile.rows]
    return factor * (1.0 / PLANAR_SCALE)


def own_blocks(tile, first, count, cells, offsets, drag, stays, acc, *scratch):
    rows = slice(first, first + count)
    sixteenths = [offsets[k, rows].astype(jnp.float32) for k in range(3)]
    force = [drag[k, rows] * stays[rows] for k in range(3)]
    return deposit_blocks(tile, cells[rows], sixteenths, force, acc, *scratch)


def first_kernel(tile, count, cells, offsets, drag, stays, acc, *scratch):
    factor = own_blocks(tile, 0, count, cells, offsets, drag, stays, acc, *scratch)
    acc[...] = acc[...] * factor


def second_kernel(tile, first, count, cells, offsets, drag, stays, acc_in, xsend, acc, *scratch):
    factor = own_blocks(tile, first, count, cells, offsets, drag, stays, acc, *scratch)
    acc[...] = acc_in[...] + acc[...] * factor


def record_row(records, row, count):
    return records[pl.ds(row, count, stride=REC), :]


def arrive_kernel(
    tile, axis, count, recv_a, recv_b, xrecv, acc_in, acc, arrivals, send_a, send_b, *scratch
):
    a_high, a_from_high = ty_roles(axis, count)

    def place(j, record):
        arrivals[j * REC : (j + 1) * REC] = record

    for i in range(3 * CAP):
        place(i, xrecv[1, i])
        place(5 * CAP + i, xrecv[0, i])

    def middle(ref, j):
        for s in range(CAP):
            place(j * CAP + s, ref[CAP + s])

    if_(
        a_from_high,
        lambda: (middle(recv_a, 4), middle(recv_b, 3)) and None,
        lambda: (middle(recv_a, 3), middle(recv_b, 4)) and None,
    )
    blocks = 8 * CAP
    live = record_row(arrivals, 10, blocks)
    force = [record_row(arrivals, k, blocks) * live for k in range(3)]
    sixteenths = [record_row(arrivals, 7 + k, blocks) for k in range(3)]
    cell = record_row(arrivals, 6, blocks).astype(jnp.int32)
    factor = deposit_blocks(tile, cell, sixteenths, force, acc, *scratch)
    acc[...] = acc_in[...] + acc[...] * factor

    def edge(ref, high):
        first = tile.ye - EDGE if high else 0
        tail = 3 * tile.edge_main
        for k in range(3):
            lanes = slice(k * tile.nz, (k + 1) * tile.nz)
            ref[k * tile.edge_main : (k + 1) * tile.edge_main] = acc[
                first * tile.wx : (first + EDGE) * tile.wx, lanes
            ]
            for h in range(2):
                start = tile.main + h * tile.hp + first
                row = tail + (2 * k + h) * EDGE
                ref[row : row + EDGE] = acc[start : start + EDGE, lanes]

    def even():
        edge(send_a, True)
        edge(send_b, False)

    def odd():
        edge(send_a, False)
        edge(send_b, True)

    for ref in (send_a, send_b):
        last = tile.edge_rows - SUB
        ref[last:] = jnp.zeros((SUB, tile.nz), jnp.float32)
    if_(a_high, even, odd)


def widen_kernel(tile, axis, count, acc, recv_a, recv_b, verticals, mid, beyond, xsend):
    _, a_from_high = ty_roles(axis, count)
    own = slice(REACH - 1, REACH - 1 + tile.ye)
    for k in range(3):
        lanes = slice(k * tile.nz, (k + 1) * tile.nz)
        zero = jnp.zeros((REACH - 1, tile.wx, tile.nz), jnp.float32)
        mid[k, : REACH - 1] = zero
        mid[k, REACH - 1 + tile.ye :] = zero
        mid[k, own] = acc[: tile.main, lanes].reshape(tile.ye, tile.wx, tile.nz)
        for h in range(2):
            start = tile.main + h * tile.hp
            beyond[k, h] = jnp.zeros((tile.yp, tile.nz), jnp.float32)
            beyond[k, h, own] = acc[start : start + tile.ye, lanes]

    def add(ref, high):
        first = tile.yw - EDGE if high else 0
        tail = 3 * tile.edge_main
        for k in range(3):
            rows = ref[k * tile.edge_main : (k + 1) * tile.edge_main]
            mid[k, first : first + EDGE] += rows.reshape(EDGE, tile.wx, tile.nz)
            for h in range(2):
                row = tail + (2 * k + h) * EDGE
                beyond[k, h, first : first + EDGE] += ref[row : row + EDGE]

    if_(
        a_from_high,
        lambda: (add(recv_a, True), add(recv_b, False)) and None,
        lambda: (add(recv_a, False), add(recv_b, True)) and None,
    )
    for k in range(3):
        for y in range(tile.yw):
            row = (k * tile.yw + y) * EDGE
            xsend[0, row : row + 1] = beyond[k, 0, y : y + 1]
            xsend[0, row + 1 : row + EDGE] = mid[k, y, :REACH]
            xsend[1, row : row + REACH] = mid[k, y, tile.wx - REACH :]
            xsend[1, row + REACH : row + EDGE] = beyond[k, 1, y : y + 1]


def stack_gas(tile, a_from_high, gas, xgas, ygas_a, ygas_b, stack):
    per_x, per_y = tile.wx // REC, tile.wy // REC

    def take_edges(ref, high):
        y = tile.ye - 1 if high else 0
        for k in range(3):
            for part in range(per_x):
                row = y * tile.wx + part * REC
                stack[k, row : row + REC] = ref[3 * CAP + k * per_x + part]
    for k in range(3):
        for h in range(2):
            start = tile.main + h * tile.hp
            stack[k, start : start + tile.hp] = jnp.zeros((tile.hp, tile.nz), jnp.float32)
            for part in range(per_y):
                row = start + 1 + part * REC
                stack[k, row : row + REC] = xgas[1 - h, 3 * CAP + k * per_y + part]
            corner = 3 * CAP + 3 * per_y
            stack[k, start : start + 1] = xgas[1 - h, corner, 2 * k : 2 * k + 1]
            last = start + tile.ye - 1
            stack[k, last : last + 1] = xgas[1 - h, corner, 2 * k + 1 : 2 * k + 2]
        for y in range(tile.wy):
            stack[k, (y + 1) * tile.wx : (y + 2) * tile.wx] = gas[
                pl.ds(k * tile.wx * tile.wy + y, tile.wx, stride=tile.wy), :
            ]
    if_(
        a_from_high,
        lambda: (take_edges(ygas_a, True), take_edges(ygas_b, False)) and None,
        lambda: (take_edges(ygas_a, False), take_edges(ygas_b, True)) and None,
    )


def tables_kernel(
    tile, axis, count, slots, cells, offsets, arrivals, gas, xgas, ygas_a, ygas_b,
    tables, tables8, verticals, stack, fields, columns,
):
    blocks = 8 * CAP
    tile.prepare(0, cells[...], [offsets[k].astype(jnp.float32) for k in range(3)], fields, columns)
    sixteenths = [record_row(arrivals, 7 + k, blocks) for k in range(3)]
    cell = record_row(arrivals, 6, blocks).astype(jnp.int32)
    tile.prepare(slots, cell, sixteenths, fields, columns)

    def build(pair, carry):
        for i in range(2):
            slot = pair * 2 + i
            row = 0
            for part in tile.planar(fields, slot):
                top, low = halves(part)
                height = part.shape[0]
                tables[slot, row : row + height] = top
                if row < COARSE:
                    tables8[slot, row : row + height] = part.astype(F8)
                    tables8[slot, COARSE + row : COARSE + row + height] = low.astype(F8)
                else:
                    down = tile.rows - COARSE + row
                    tables[slot, down : down + height] = low.astype(jnp.bfloat16)
                row += height
            verticals[slot], _ = tile.vertical(columns, slot)
        return carry

    lax.fori_loop(0, (slots + blocks) // 2, build, 0)
    _, a_from_high = ty_roles(axis, count)
    stack_gas(tile, a_from_high, gas, xgas, ygas_a, ygas_b, stack)


def finish_kernel(
    tile, slots, stays, velocity, arrivals, tables, tables8, verticals, stack,
    mid, beyond, xrecv, gas_out, slip, src, ping, pong, field, field8, ext, gas_new, sem,
):
    zero = SUB + SWEEPS
    after = zero + tile.wx
    swept = tile.wx + 2 * SWEEPS
    for k in range(3):
        for y in range(tile.yw):
            row = (k * tile.yw + y) * EDGE
            src[k, y, zero - REACH : zero - 1] = xrecv[1, row : row + REACH - 1]
            src[k, y, zero - 1 : zero] = xrecv[1, row + REACH - 1 : row + REACH] + beyond[k, 0, y : y + 1]
            src[k, y, zero:after] = mid[k, y]
            src[k, y, zero : zero + 1] += xrecv[1, row + REACH : row + EDGE]
            src[k, y, after - 1 : after] += xrecv[0, row : row + 1]
            src[k, y, after : after + 1] = xrecv[0, row + 1 : row + 2] + beyond[k, 1, y : y + 1]
            src[k, y, after + 1 : after + REACH] = xrecv[0, row + 2 : row + EDGE]

    def sweep(old, new, margin):
        def row(y):
            for k in range(3):
                here = old[k, y, SUB : SUB + swept]
                around = old[k, y - 1, SUB : SUB + swept] + old[k, y + 1, SUB : SUB + swept]
                around = around + old[k, y, SUB - 1 : SUB - 1 + swept]
                around = around + old[k, y, SUB + 1 : SUB + 1 + swept]
                around = around + pltpu.roll(here, 1, 1) + pltpu.roll(here, tile.nz - 1, 1)
                total = src[k, y, SUB : SUB + swept] + DIFFUSE * around
                new[k, y, SUB : SUB + swept] = total * (1.0 / (1.0 + 6.0 * DIFFUSE))

        for y in range(margin, tile.yw - margin):
            row(y)

    buffers = [src, ping, pong, ping, pong]
    for index in range(SWEEPS):
        sweep(buffers[index], buffers[index + 1], index + 1)
    filtered = buffers[SWEEPS]

    for k in range(3):
        ext[k, tile.main :] = stack[k, tile.main :]
        for y in range(tile.ye):
            rows = slice(y * tile.wx, (y + 1) * tile.wx)
            updated = stack[k, rows] + STEP_SIZE * filtered[k, y + REACH - 1, zero:after]
            ext[k, rows] = updated
            if 1 <= y <= tile.wy:
                gas_new[pl.ds(k * tile.wx * tile.wy + y - 1, tile.wx, stride=tile.wy), :] = updated
            for h, x in ((0, zero - 1), (1, after)):
                row = tile.main + h * tile.hp + y
                ext[k, row : row + 1] += STEP_SIZE * filtered[k, y + REACH - 1, x : x + 1]
    leave = pltpu.make_async_copy(gas_new, gas_out, sem)
    leave.start()
    blocks = 8 * CAP
    total = slots + blocks
    fine = tile.rows - COARSE
    pad_rows = round_up(3 * fine, 128) - 3 * fine
    values, factor = scaled([ext[k] for k in range(3)], 1.0)
    for k, value in enumerate(values):
        top = value.astype(jnp.bfloat16).astype(jnp.float32)
        low = value - top
        pad = jnp.zeros((pad_rows, tile.nz), jnp.float32)
        exact = jnp.concatenate([top, top[COARSE:], low[COARSE:], pad], axis=0).T
        cross = jnp.concatenate([low[:COARSE], value[:COARSE]], axis=0).T
        rows = slice(k * tile.nz, (k + 1) * tile.nz)
        for i in range(field.shape[0]):
            field[i, rows] = exact[:, i * 128 : (i + 1) * 128].astype(jnp.bfloat16)
        for i in range(field8.shape[0]):
            field8[i, rows] = cross[:, i * 128 : (i + 1) * 128].astype(F8)
    factor = factor * (1.0 / PLANAR_SCALE)

    def sample(pair, carry):
        pad = jnp.zeros((pad_rows, 128), jnp.bfloat16)
        slabs = [tables[pair * 2 + i] for i in range(2)]
        slabs = [jnp.concatenate([slab, slab[COARSE : tile.rows], pad], axis=0) for slab in slabs]
        column = jnp.dot(
            jnp.concatenate([field[i] for i in range(field.shape[0])], axis=1),
            jnp.concatenate(slabs, axis=1),
            preferred_element_type=jnp.float32,
        )
        column = column + jnp.dot(
            jnp.concatenate([field8[i] for i in range(field8.shape[0])], axis=1),
            jnp.concatenate([tables8[pair * 2 + i] for i in range(2)], axis=1),
            preferred_element_type=jnp.float32,
        )
        for i in range(2):
            vertical = verticals[pair * 2 + i]
            for k in range(3):
                part = column[k * tile.nz : (k + 1) * tile.nz, i * 128 : (i + 1) * 128]
                value = jnp.sum(part * vertical, axis=0, keepdims=True)
                slip[k, pl.ds(pair * 2 + i, 1)] = value
        return carry

    lax.fori_loop(0, total // 2, sample, 0, unroll=True)
    live = record_row(arrivals, 10, blocks)
    for k in range(3):
        slip[k, :slots] = (slip[k, :slots] * factor - velocity[k]) * stays[...]
        slip[k, slots:] = (slip[k, slots:] * factor - record_row(arrivals, 3 + k, blocks)) * live
    leave.wait()


def exchange_x(buffer, axis, count):
    forward = [(i, (i + 1) % count) for i in range(count)]
    backward = [(target, source) for source, target in forward]
    if count == 2:
        return lax.ppermute(buffer, axis, forward)
    return jnp.stack(
        [lax.ppermute(buffer[0], axis, backward), lax.ppermute(buffer[1], axis, forward)]
    )


def exchange_y(send_a, send_b, axis, count):
    if count % 2:
        perm_a = [(i, (i + 1) % count) for i in range(count)]
        perm_b = [(target, source) for source, target in perm_a]
    else:
        perm_a = [(i, i ^ 1) for i in range(count)]
        perm_b = [(i, (i + 1) % count if i % 2 else (i - 1) % count) for i in range(count)]
    return lax.ppermute(send_a, axis, perm_a), lax.ppermute(send_b, axis, perm_b)


def on_device(count_x, count_y, handoff, cells, offsets, drag, bubble_velocity, gas):
    tile = Tile(gas.shape[1], gas.shape[2], gas.shape[3])
    slots, lanes = cells.shape[2], cells.shape[3]
    codes = handoff.reshape(slots)
    cells = cells.reshape(slots, lanes)
    offsets = offsets.reshape(slots, 3, lanes).transpose(1, 0, 2)
    drag = drag.reshape(slots, 3, lanes).transpose(1, 0, 2)
    velocity = bubble_velocity.reshape(slots, 3, lanes).transpose(1, 0, 2)
    gas_rows = gas.reshape(3 * tile.wx * tile.wy, tile.nz)
    per_x, per_y = tile.wx // REC, tile.wy // REC
    bind = functools.partial
    macs = tile.rows * 3 * tile.nz * 3 * 2 * lanes

    inputs = [cells, offsets, drag, velocity, gas_rows]
    ty_shape = (3 * CAP + 3 * per_x, REC, lanes)
    send_a, send_b, own, stays, cells, offsets, drag, velocity, gas_rows = call(
        bind(pack_kernel, tile, "ty", count_y, slots),
        [ty_shape, ty_shape, (2, CAP, REC, lanes), (slots, lanes)]
        + [(value.shape, value.dtype) for value in inputs],
        [codes, *inputs],
        [HBM] * 6,
        scratch=[
            pltpu.SMEM((slots,), jnp.int32),
            pltpu.SMEM((slots + 1,), jnp.int32),
            pltpu.SMEM((9,), jnp.int32),
            pltpu.SemaphoreType.DMA((6,)),
        ],
        name="pack",
    )
    recv_a, recv_b = exchange_y(send_a, send_b, "ty", count_y)
    cut = slots * 2 // 3 // 4 * 4
    (acc,) = call(
        bind(first_kernel, tile, cut),
        [(tile.rows, 3 * tile.nz)],
        [cells, offsets, drag, stays],
        scratch=table_scratch(tile, cut),
        cost=(macs * cut, cut * lanes * 40),
        name="deposit_first",
    )
    (xsend,) = call(
        bind(join_kernel, tile, "ty", count_y),
        [(2, 3 * CAP + 3 * per_y + 1, REC, lanes)],
        [recv_a, recv_b, own, gas_rows, acc],
        [VMEM] * 4 + [ANY],
        name="join",
    )
    xrecv = exchange_x(xsend, "tx", count_x)
    (acc,) = call(
        bind(second_kernel, tile, cut, slots - cut),
        [acc.shape],
        [cells, offsets, drag, stays, acc, xsend],
        [VMEM] * 5 + [ANY],
        scratch=table_scratch(tile, slots - cut),
        cost=(macs * (slots - cut), (slots - cut) * lanes * 40),
        name="deposit_second",
    )
    edge_shape = (tile.edge_rows, tile.nz)
    blocks = 8 * CAP
    acc, arrivals, edge_a, edge_b = call(
        bind(arrive_kernel, tile, "ty", count_y),
        [acc.shape, (blocks * REC, lanes), edge_shape, edge_shape],
        [recv_a, recv_b, xrecv, acc],
        scratch=table_scratch(tile, blocks),
        cost=(macs * blocks, blocks * lanes * 40),
        name="deposit_arrivals",
    )
    got_a, got_b = exchange_y(edge_a, edge_b, "ty", count_y)
    total = slots + blocks
    fine = tile.rows - COARSE
    tables, tables8, verticals, stack = call(
        bind(tables_kernel, tile, "ty", count_y, slots),
        [
            ((total, tile.rows + fine, lanes), jnp.bfloat16),
            ((total, 2 * COARSE, lanes), F8),
            (total, tile.nz, lanes),
            (3, tile.rows, tile.nz),
        ],
        [cells, offsets, arrivals, gas_rows, xrecv, recv_a, recv_b],
        scratch=[
            pltpu.VMEM((8, total, lanes), jnp.float32),
            pltpu.VMEM((total * COLS, lanes), jnp.float32),
        ],
        cost=(macs * total // 2, total * lanes * 40),
        name="tables",
    )
    mid, beyond, xedge = call(
        bind(widen_kernel, tile, "ty", count_y),
        [
            (3, tile.yw, tile.wx, tile.nz),
            (3, 2, tile.yp, tile.nz),
            (2, round_up(3 * tile.yw * EDGE, SUB), tile.nz),
        ],
        [acc, got_a, got_b, verticals],
        [VMEM] * 3 + [ANY],
        name="widen",
    )
    xgot = exchange_x(xedge, "tx", count_x)
    wide = (3, tile.yw, round_up(tile.wx + SUB + SWEEPS + SUB, SUB), tile.nz)
    gas_new, slip = call(
        bind(finish_kernel, tile, slots),
        [gas_rows.shape, (3, total, lanes)],
        [stays, velocity, arrivals, tables, tables8, verticals, stack, mid, beyond, xgot],
        scratch=[
            *[pltpu.VMEM(wide, jnp.float32)] * 3,
            pltpu.VMEM(((COARSE + round_up(3 * fine, 128)) // 128, 3 * tile.nz, 128), jnp.bfloat16),
            pltpu.VMEM((2 * COARSE // 128, 3 * tile.nz, 128), F8),
            pltpu.VMEM((3, tile.rows, tile.nz), jnp.float32),
            pltpu.VMEM(gas_rows.shape, jnp.float32),
            pltpu.SemaphoreType.DMA(()),
        ],
        out_specs=[HBM, VMEM],
        cost=(macs * total, total * lanes * 40),
        name="finish",
        results=True,
    )
    return gas_new.reshape(gas.shape), slip.transpose(1, 0, 2).reshape(1, 1, total, 3, lanes)


def solution(mesh):
    return jax.shard_map(
        functools.partial(on_device, mesh.shape["tx"], mesh.shape["ty"]),
        mesh=mesh,
        in_specs=(
            P("tx", "ty", None, None),
            P("tx", "ty", None, None),
            P("tx", "ty", None, None, None),
            P("tx", "ty", None, None, None),
            P("tx", "ty", None, None, None),
            P(None, "tx", "ty", None),
        ),
        out_specs=(P(None, "tx", "ty", None), P("tx", "ty", None, None, None)),
        check_vma=False,
    )
```
